32 devices in a mesh: pts: 8 (over y, x, core), cen: 4 (over z).
Axes of the slice: x: 2, y: 2, z: 4, core: 2. Of those that a mesh axis runs over, the one named last changes fastest.
Arguments:
- embeddings: float32 [8192, 64], P('pts'), may hold values from -0.75 to 0.75
- centroids: float32 [8192, 64], P('cen'), may hold values from -0.75 to 0.75
- point_duals: float32 [8192], P('pts'), may hold values from -4 to 0.1
- centroid_duals: float32 [8192], P('cen'), may hold values from -1.5 to 2.6
- targets: float32 [8192, 64], P('pts'), may hold values from -6 to 6
Outputs:
- grad_emb: float32 [8192, 64], P('pts')
- grad_cen: float32 [8192, 64], P(('cen', 'pts'))
The draws below stay inside these ranges and needn't reach their ends.
All inputs are finite; a program needn't handle non-finite values.
Results may differ from the reference program's by a relative error of at most 0.0003.
Values sent between devices are 32-bit elements; how exact they have to be, the bound alone decides.
No kernel may reach another device: no remote copies, remote signals or barrier semaphores. Data moves between devices by JAX's collectives and lax.ppermute only.
A program may use at most 64 MiB of HBM per device.

```python
import jax
import jax.numpy as jnp
from jax import lax

WIDTH = 64
ITERS = 3
POINTS = 8192
CENTROIDS = 8192


def draw_point_duals(key, part):
    position = jnp.arange(POINTS, dtype=jnp.float32) / POINTS
    base = jax.random.uniform(key, (POINTS,), jnp.float32, -4.0, -1.0)
    return base + 1.1 * position


def draw_centroid_duals(key, part):
    position = jnp.arange(CENTROIDS, dtype=jnp.float32) / CENTROIDS
    base = jax.random.uniform(key, (CENTROIDS,), jnp.float32, -1.5, 1.5)
    return base + 1.1 * position


def steps_of(key, extent, split, low, high):
    def one(axis_at, shards_of):
        draws = jax.random.uniform(jax.random.fold_in(jax.random.fold_in(key, 6), axis_at), (shards_of,), jnp.float32, low / len(split), high / len(split))
        return jnp.repeat(jnp.exp(draws), extent[axis_at] // shards_of).reshape((-1,) + (1,) * (len(extent) - axis_at - 1))

    loudness = one(*split[0])
    for cut in split[1:]:
        loudness = loudness * one(*cut)
    return loudness


def scatter_about(own_key, dims, deviation, limit, pieces=(), kind=jnp.bfloat16):
    loudness = steps_of(own_key, dims, pieces, -0.22, 0.18) if pieces else 1.0
    array = jax.random.normal(own_key, dims, jnp.float32) * deviation * loudness
    return jnp.minimum(jnp.maximum(array, -limit), limit).astype(kind)


def setup_inputs(seed: int = 0) -> dict:
    keys = jax.random.split(jax.random.key(seed), 6)
    embeddings = scatter_about(keys[0], (POINTS, WIDTH), 0.125, 0.75, ((0, 8),), jnp.float32)
    centroids = scatter_about(keys[1], (CENTROIDS, WIDTH), 0.125, 0.75, ((0, 4),), jnp.float32)
    point_duals = draw_point_duals(jax.random.fold_in(keys[5], 71), 0)
    centroid_duals = draw_centroid_duals(jax.random.fold_in(keys[5], 71), 0)
    targets = scatter_about(keys[4], (POINTS, WIDTH), 1.0, 6.0, ((0, 8),), jnp.float32)
    return dict(embeddings=embeddings, centroids=centroids, point_duals=point_duals, centroid_duals=centroid_duals, targets=targets)


EPSILON = 0.08


def plan_block(points, duals_row, cen_block, duals_block, plan_total):
    scores = jnp.dot(points, cen_block.T, precision=lax.Precision.HIGHEST, preferred_element_type=jnp.float32)
    return jnp.exp(duals_row[:, None] + duals_block[None, :] + scores / EPSILON) / plan_total


def reference(embeddings, centroids, point_duals, centroid_duals, targets):
    exact_mode = lax.Precision.HIGHEST
    feat_width = centroids.shape[1]
    block_cols = min(1024, CENTROIDS)
    block_count = CENTROIDS // block_cols
    plan_total = float(CENTROIDS)
    cen_blocks = centroids.reshape(block_count, block_cols, feat_width)
    dual_blocks = centroid_duals.reshape(block_count, block_cols)
    rows_zero = jnp.zeros((POINTS,), jnp.float32)

    def first_step(running, inputs):
        cen_block, duals_block = inputs
        plan_tile = plan_block(embeddings, point_duals, cen_block, duals_block, plan_total)
        target_scores = jnp.dot(targets, cen_block.T, precision=exact_mode, preferred_element_type=jnp.float32)
        weighted = plan_tile * target_scores
        return (running[0] + plan_tile.sum(1), running[1] + weighted.sum(1)), (plan_tile.sum(0), weighted.sum(0))

    (row_mass, row_load), (col_mass, col_load) = lax.scan(first_step, (rows_zero, rows_zero), (cen_blocks, dual_blocks))
    col_mass = col_mass.reshape(-1)
    col_load = col_load.reshape(-1)
    alpha = row_load
    beta = col_load
    for sweep_turn in range(ITERS):
        row_scale = alpha / row_mass
        scale_blocks = (beta / col_mass).reshape(block_count, block_cols)

        def sweep_step(running, inputs):
            cen_block, duals_block, scale_block = inputs
            plan_tile = plan_block(embeddings, point_duals, cen_block, duals_block, plan_total)
            row_part = jnp.dot(plan_tile, scale_block, precision=exact_mode, preferred_element_type=jnp.float32)
            col_part = jnp.dot(row_scale, plan_tile, precision=exact_mode, preferred_element_type=jnp.float32)
            return running + row_part, col_part

        row_terms, col_terms = lax.scan(sweep_step, rows_zero, (cen_blocks, dual_blocks, scale_blocks))
        alpha = row_load - row_terms
        beta = col_load - col_terms.reshape(-1)
    row_scale = alpha / row_mass
    scale_blocks = (beta / col_mass).reshape(block_count, block_cols)

    def final_step(running, inputs):
        cen_block, duals_block, scale_block = inputs
        plan_tile = plan_block(embeddings, point_duals, cen_block, duals_block, plan_total)
        target_scores = jnp.dot(targets, cen_block.T, precision=exact_mode, preferred_element_type=jnp.float32)
        weights = plan_tile * (target_scores - row_scale[:, None] - scale_block[None, :])
        emb_part = jnp.dot(weights, cen_block, precision=exact_mode, preferred_element_type=jnp.float32)
        cen_part = lax.dot_general(weights, embeddings, (((0,), (0,)), ((), ())), precision=exact_mode, preferred_element_type=jnp.float32)
        return running + emb_part, cen_part

    emb_zero = jnp.zeros((POINTS, feat_width), jnp.float32)
    grad_emb, cen_parts = lax.scan(final_step, emb_zero, (cen_blocks, dual_blocks, scale_blocks))
    return grad_emb, cen_parts.reshape(CENTROIDS, feat_width)
```

```python
import math

import jax
import jax.numpy as jnp
from jax import lax
from jax.experimental import pallas as pl
from jax.experimental.pallas import tpu as pltpu
from jax.sharding import PartitionSpec as P

EPSILON = 0.08
LANES = 128
F32 = jnp.float32
BF16 = jnp.bfloat16
VMEM = pl.BlockSpec(memory_space=pltpu.VMEM)
SMEM = pl.BlockSpec(memory_space=pltpu.SMEM)


def split2(x):
    high = x.astype(BF16)
    low = (x - high.astype(F32)).astype(BF16)
    return high, low


def split3(x):
    high = x.astype(BF16)
    rest = x - high.astype(F32)
    mid = rest.astype(BF16)
    low = (rest - mid.astype(F32)).astype(BF16)
    return high, mid, low


def dot_nt(a, b):
    return lax.dot_general(a, b, (((1,), (1,)), ((), ())), preferred_element_type=F32)


def spread_rows(row):
    return jnp.broadcast_to(row, (LANES, LANES)).T


def gather_rows(block):
    return jnp.sum(block.T, axis=0, keepdims=True)


def dual_lanes(dual, own_first):
    blocks = []
    lane = lax.broadcasted_iota(jnp.int32, (LANES, LANES), 1)
    lane = lane if own_first else (lane + 3) % 6 + (lane // 6) * 6
    for g in range(dual.shape[0]):
        high, mid, low = (part.astype(F32) for part in split3(spread_rows(dual[g : g + 1, :])))
        ones = jnp.where(lane < 6, 1.0, 0.0)
        block = jnp.where(lane == 0, high, jnp.where(lane == 1, mid, jnp.where(lane == 2, low, ones)))
        blocks.append(block[:, :64].astype(BF16))
    return jnp.concatenate(blocks, axis=0)


def first_kernel(total, emb_ref, tgt_ref, cen_ref, pd_ref, cd_ref, plan_ref, cot_ref, rows_ref, cols_ref,
                 lhs_ref, tlhs_ref, rhs_ref, rm_ref, rl_ref, cm_ref, cl_ref):
    rows, cols = plan_ref.shape
    eh, el = split2(emb_ref[...] * (1.0 / EPSILON))
    lhs_ref[...] = jnp.concatenate([eh, eh, el, dual_lanes(pd_ref[...], True)], axis=1)
    th, tl = split2(tgt_ref[...])
    tlhs_ref[...] = jnp.concatenate([th, th, tl, jnp.zeros_like(th)], axis=1)
    ch, cl = split2(cen_ref[...])
    shifted = cd_ref[...] - math.log(total)
    rhs_ref[...] = jnp.concatenate([ch, cl, ch, dual_lanes(shifted, False)], axis=1)
    cm_ref[...] = jnp.zeros_like(cm_ref)
    cl_ref[...] = jnp.zeros_like(cl_ref)
    tm, tn = 128, 256

    @pl.loop(0, rows // tm)
    def _(i):
        at = pl.ds(pl.multiple_of(i * tm, tm), tm)
        left = lhs_ref[at, :]
        tleft = tlhs_ref[at, :]
        mass = jnp.zeros((tm, LANES), F32)
        load = jnp.zeros((tm, LANES), F32)
        for j in range(cols // tn):
            js = slice(j * tn, (j + 1) * tn)
            right = rhs_ref[js, :]
            plan = jnp.exp(dot_nt(left, right))
            cot = dot_nt(tleft, right)
            plan_ref[at, js] = plan
            cot_ref[at, js] = cot
            weighted = plan * cot
            for h in range(tn // LANES):
                hs = slice(h * LANES, (h + 1) * LANES)
                mass = mass + plan[:, hs]
                load = load + weighted[:, hs]
            cm_ref[:, js] += jnp.sum(plan.reshape(tm // 8, 8, tn), axis=0)
            cl_ref[:, js] += jnp.sum(weighted.reshape(tm // 8, 8, tn), axis=0)
        rm_ref[at, :] = mass
        rl_ref[at, :] = load

    groups = rows // LANES
    for g in range(groups):
        gs = slice(g * LANES, (g + 1) * LANES)
        rows_ref[g : g + 1, :] = gather_rows(rm_ref[gs, :])
        rows_ref[groups + g : groups + g + 1, :] = gather_rows(rl_ref[gs, :])
    tiles = cols // LANES
    for t in range(tiles):
        ts = slice(t * LANES, (t + 1) * LANES)
        cols_ref[t : t + 1, :] = jnp.sum(cm_ref[:, ts], axis=0, keepdims=True)
        cols_ref[tiles + t : tiles + t + 1, :] = jnp.sum(cl_ref[:, ts], axis=0, keepdims=True)


def columns_of(plan_ref, scales, spread_ref, out_ref):
    rows, cols = plan_ref.shape
    tiles = cols // LANES
    count = len(scales)
    for k, scale in enumerate(scales):
        for g in range(rows // LANES):
            spread_ref[k, g * LANES : (g + 1) * LANES, :] = spread_rows(scale[g : g + 1, :])
    wide = 16 // count
    for t0 in range(0, tiles, wide):
        span = min(wide, tiles - t0)

        def step(i, acc, t0=t0, span=span):
            acc = list(acc)
            for r in range(2):
                at = pl.ds(pl.multiple_of(i * 16 + r * 8, 8), 8)
                scale_rows = [spread_ref[k, at, :] for k in range(count)]
                for t in range(span):
                    tile = plan_ref[at, (t0 + t) * LANES : (t0 + t + 1) * LANES]
                    for k in range(count):
                        acc[k * span + t] = acc[k * span + t] + tile * scale_rows[k]
            return tuple(acc)

        zero = jnp.zeros((8, LANES), F32)
        acc = lax.fori_loop(0, rows // 16, step, (zero,) * (count * span))
        for k in range(count):
            for t in range(span):
                at = k * tiles + t0 + t
                out_ref[at : at + 1, :] = jnp.sum(acc[k * span + t], axis=0, keepdims=True)


def rows_of(plan_ref, scales, part_ref, out_ref):
    rows, cols = plan_ref.shape
    tiles = cols // LANES
    groups = rows // LANES
    count = len(scales)
    spread = [
        [jnp.broadcast_to(scale[t : t + 1, :], (8, LANES)) for t in range(tiles)] for scale in scales
    ]

    @pl.loop(0, rows // 16)
    def _(i):
        for r in range(2):
            at = pl.ds(pl.multiple_of(i * 16 + r * 8, 8), 8)
            sums = [[None, None] for _ in range(count)]
            for t in range(tiles):
                tile = plan_ref[at, t * LANES : (t + 1) * LANES]
                for k in range(count):
                    term = tile * spread[k][t]
                    old = sums[k][t % 2]
                    sums[k][t % 2] = term if old is None else old + term
            for k in range(count):
                one, two = sums[k]
                part_ref[k, at, :] = one if two is None else one + two

    for k in range(count):
        for g in range(groups):
            at = k * groups + g
            out_ref[at : at + 1, :] = gather_rows(part_ref[k, g * LANES : (g + 1) * LANES, :])


def second_kernel(plan_ref, rows_ref, cols_ref, out_ref, own_ref, spread_ref):
    groups = rows_ref.shape[0] // 2
    tiles = own_ref.shape[0]
    scale = rows_ref[groups:, :] / rows_ref[:groups, :]
    columns_of(plan_ref, [scale], spread_ref, own_ref)
    out_ref[: 2 * tiles, :] = cols_ref[...]
    out_ref[2 * tiles :, :] = own_ref[...]


def third_kernel(plan_ref, cols_ref, out_ref, part_ref):
    tiles = cols_ref.shape[0] // 3
    mass = cols_ref[:tiles, :]
    load = cols_ref[tiles : 2 * tiles, :]
    beta = load - cols_ref[2 * tiles :, :]
    rows_of(plan_ref, [load / mass, beta / mass], part_ref, out_ref)


def fourth_kernel(plan_ref, rows_ref, terms_ref, out_ref, spread_ref):
    groups = rows_ref.shape[0] // 2
    mass = rows_ref[:groups, :]
    load = rows_ref[groups:, :]
    scales = [(load - terms_ref[k * groups : (k + 1) * groups, :]) / mass for k in range(2)]
    columns_of(plan_ref, scales, spread_ref, out_ref)


def fifth_kernel(plan_ref, cols_ref, terms_ref, out_ref, part_ref):
    tiles = cols_ref.shape[0] // 3
    beta = cols_ref[tiles : 2 * tiles, :] - terms_ref[:tiles, :]
    rows_of(plan_ref, [beta / cols_ref[:tiles, :]], part_ref, out_ref)


def final_kernel(order_ref, plan_ref, cot_ref, emb_ref, cen_ref, rows_ref, aterms_ref, cols_ref, bterms_ref,
                 gemb_ref, gcen_ref, right_ref, left_ref, spread_ref, acc_ref):
    rows, cols = plan_ref.shape
    groups = rows // LANES
    tiles = cols // LANES
    mass = rows_ref[:groups, :]
    alpha = (rows_ref[groups:, :] - aterms_ref[...]) / mass
    for g in range(groups):
        spread_ref[g * LANES : (g + 1) * LANES, :] = spread_rows(alpha[g : g + 1, :])
    beta = (cols_ref[tiles : 2 * tiles, :] - bterms_ref[tiles:, :]) / cols_ref[:tiles, :]
    ch, cl = split2(cen_ref[...])
    right_ref[...] = jnp.concatenate([ch, cl], axis=1)
    eh, el = split2(emb_ref[...])
    both = jnp.concatenate([eh.astype(F32), el.astype(F32)], axis=1)
    for g in range(groups):
        left_ref[:, g * LANES : (g + 1) * LANES] = both[g * LANES : (g + 1) * LANES, :].T.astype(BF16)
    acc_ref[...] = jnp.zeros_like(acc_ref)
    tn = 256
    tm = 256
    emb_chunks = gemb_ref.shape[0]
    emb_rows = gemb_ref.shape[1]
    half = rows // 2
    cen_chunks, _, chunk_cols = gcen_ref.shape
    for j in range(cols // tn):
        js = slice(j * tn, (j + 1) * tn)
        lows = [
            jnp.broadcast_to(beta[t : t + 1, :], (8, LANES))
            for t in range(j * tn // LANES, (j + 1) * tn // LANES)
        ]
        low = jnp.concatenate(lows, axis=1)
        gcen = jnp.zeros((LANES, tn), F32)
        for i in range(rows // tm):
            at = slice(i * tm, (i + 1) * tm)
            shift = jnp.tile(spread_ref[at, :], (1, tn // LANES)).reshape(tm // 8, 8, tn) + low[None]
            weights = plan_ref[at, js] * (cot_ref[at, js] - shift.reshape(tm, tn))
            wh, wl = split2(weights)
            right = right_ref[js, :]
            acc_ref[at, :] += jnp.dot(wh, right, preferred_element_type=F32) + jnp.dot(
                wl, right, preferred_element_type=F32
            )
            left = left_ref[:, at]
            gcen = (
                gcen
                + jnp.dot(left, wh, preferred_element_type=F32)
                + jnp.dot(left, wl, preferred_element_type=F32)
            )
        gcen = gcen[:64] + gcen[64:]
        span = min(chunk_cols, tn)
        for s in range(tn // span):
            col = j * tn + s * span
            gcen_ref[order_ref[0, col // chunk_cols], :, pl.ds(col % chunk_cols, span)] = gcen[
                :, s * span : (s + 1) * span
            ]
    lane = lax.broadcasted_iota(jnp.int32, (emb_rows, LANES), 1)
    for q in range(emb_chunks):
        one = acc_ref[q * emb_rows : (q + 1) * emb_rows, :]
        two = acc_ref[half + q * emb_rows : half + (q + 1) * emb_rows, :]
        one = one + pltpu.roll(one, 64, 1)
        two = two + pltpu.roll(two, 64, 1)
        gemb_ref[order_ref[1, q]] = jnp.where(lane < 64, one, two)


def last_kernel(order_ref, gemb_ref, gcen_ref, emb_ref, cen_ref):
    chunks, emb_rows, _ = gemb_ref.shape
    half = chunks * emb_rows
    for q in range(chunks):
        block = gemb_ref[order_ref[1, q]]
        emb_ref[q * emb_rows : (q + 1) * emb_rows, :] = block[:, :64]
        emb_ref[half + q * emb_rows : half + (q + 1) * emb_rows, :] = block[:, 64:]
    cen_ref[...] = gcen_ref[0].T


def bits_of(count):
    return [1 << b for b in range(count.bit_length() - 1)]


def swap(value, axis, count, bit):
    return lax.ppermute(value, axis, [(i, i ^ bit) for i in range(count)])


def sum_all(value, axis, count):
    for bit in bits_of(count):
        value = value + swap(value, axis, count, bit)
    return value


def place_of(count):
    bits = bits_of(count)
    return [sum(((k >> b) & 1) << (len(bits) - 1 - b) for b in range(len(bits))) for k in range(count)]


def order_table(axis, count, size):
    me = lax.axis_index(axis)
    place = jnp.array(place_of(count), jnp.int32)
    row = place[jnp.arange(count, dtype=jnp.int32) ^ me]
    return jnp.pad(row, (0, size - count))


def shards(embeddings, centroids, point_duals, centroid_duals, targets):
    pts = lax.axis_size("pts")
    cen = lax.axis_size("cen")
    rows, width = embeddings.shape
    cols = centroids.shape[0]
    groups, tiles = rows // LANES, cols // LANES
    size = max(pts, cen)
    order = jnp.stack([order_table("pts", pts, size), order_table("cen", cen, size)])
    sds = jax.ShapeDtypeStruct

    def call(body, name, outs, scratch, mib, specs, *args):
        return pl.pallas_call(
            body,
            name=name,
            out_shape=outs,
            in_specs=specs,
            out_specs=jax.tree.map(lambda _: VMEM, outs),
            scratch_shapes=scratch,
            compiler_params=pltpu.CompilerParams(vmem_limit_bytes=mib << 20),
        )(*args)

    def first(*args):
        return first_kernel(float(cols * cen), *args)

    plan, cot, row_sums, col_sums = call(
        first,
        "first",
        (
            pltpu.VMEM((rows, cols), F32),
            pltpu.VMEM((rows, cols), F32),
            sds((2 * groups, LANES), F32),
            sds((2 * tiles, LANES), F32),
        ),
        [
            pltpu.VMEM((rows, 256), BF16),
            pltpu.VMEM((rows, 256), BF16),
            pltpu.VMEM((cols, 256), BF16),
            pltpu.VMEM((rows, LANES), F32),
            pltpu.VMEM((rows, LANES), F32),
            pltpu.VMEM((8, cols), F32),
            pltpu.VMEM((8, cols), F32),
        ],
        40,
        [VMEM] * 5,
        embeddings,
        targets,
        centroids,
        point_duals.reshape(groups, LANES),
        centroid_duals.reshape(tiles, LANES),
    )
    row_sums = sum_all(row_sums, "cen", cen)
    col_all = call(
        second_kernel,
        "second",
        sds((3 * tiles, LANES), F32),
        [pltpu.VMEM((tiles, LANES), F32), pltpu.VMEM((1, rows, LANES), F32)],
        16,
        [VMEM] * 3,
        plan,
        row_sums,
        col_sums,
    )
    col_all = sum_all(col_all, "pts", pts)
    row_terms = call(
        third_kernel,
        "third",
        sds((2 * groups, LANES), F32),
        [pltpu.VMEM((2, rows, LANES), F32)],
        16,
        [VMEM] * 2,
        plan,
        col_all,
    )
    row_terms = sum_all(row_terms, "cen", cen)
    col_terms = call(
        fourth_kernel,
        "fourth",
        sds((2 * tiles, LANES), F32),
        [pltpu.VMEM((2, rows, LANES), F32)],
        16,
        [VMEM] * 3,
        plan,
        row_sums,
        row_terms,
    )
    col_terms = sum_all(col_terms, "pts", pts)
    last_terms = call(
        fifth_kernel,
        "fifth",
        sds((groups, LANES), F32),
        [pltpu.VMEM((1, rows, LANES), F32)],
        16,
        [VMEM] * 3,
        plan,
        col_all,
        col_terms,
    )
    last_terms = sum_all(last_terms, "cen", cen)
    gemb, gcen = call(
        final_kernel,
        "final",
        (sds((cen, rows // 2 // cen, LANES), F32), sds((pts, width, cols // pts), F32)),
        [
            pltpu.VMEM((cols, LANES), BF16),
            pltpu.VMEM((LANES, rows), BF16),
            pltpu.VMEM((rows, LANES), F32),
            pltpu.VMEM((rows, LANES), F32),
        ],
        40,
        [SMEM] + [VMEM] * 8,
        order,
        plan,
        cot,
        embeddings,
        centroids,
        row_sums,
        last_terms,
        col_all,
        col_terms,
    )
    cbits, pbits = bits_of(cen), bits_of(pts)
    for bit in pbits:
        keep = gcen.shape[0] // 2
        gcen = gcen[:keep] + swap(gcen[keep:], "pts", pts, bit)
    for bit in cbits:
        keep = gemb.shape[0] // 2
        gemb = gemb[:keep] + swap(gemb[keep:], "cen", cen, bit)
    for bit in reversed(cbits):
        gemb = jnp.concatenate([gemb, swap(gemb, "cen", cen, bit)], axis=0)
    return call(
        last_kernel,
        "last",
        (sds((rows, width), F32), sds((cols // pts, width), F32)),
        [],
        16,
        [SMEM] + [VMEM] * 2,
        order,
        gemb,
        gcen,
    )


def solution(mesh):
    in_specs = (P("pts", None), P("cen", None), P("pts"), P("cen"), P("pts", None))
    out_specs = (P("pts", None), P(("cen", "pts"), None))
    return jax.shard_map(shards, mesh=mesh, in_specs=in_specs, out_specs=out_specs, check_vma=False)
```

```python
import math

import jax
import jax.numpy as jnp
from jax import lax
from jax.experimental import pallas as pl
from jax.experimental.pallas import tpu as pltpu
from jax.sharding import PartitionSpec as P


EPSILON = 0.08
LANES = 128
F32 = jnp.float32
BF16 = jnp.bfloat16
VMEM = pl.BlockSpec(memory_space=pltpu.VMEM)


def bits_of(count):
    return [1 << b for b in range(count.bit_length() - 1)]


def reverse_bits(k, count):
    size = len(bits_of(count))
    return sum(((k >> b) & 1) << (size - 1 - b) for b in range(size))


def split2(x):
    high = x.astype(BF16)
    low = (x - high.astype(F32)).astype(BF16)
    return high, low


def split3(x):
    high = x.astype(BF16)
    rest = x - high.astype(F32)
    mid = rest.astype(BF16)
    low = (rest - mid.astype(F32)).astype(BF16)
    return high, mid, low


def dot(a, b):
    return jnp.dot(a, b, preferred_element_type=F32)


def flat_row(blocks, out_ref):
    for g in range(blocks.shape[0]):
        out_ref[:, g * LANES : (g + 1) * LANES] = blocks[g : g + 1, :]


def transpose_into(out_ref, source, out_at=0):
    for g in range(source.shape[1] // LANES):
        gs = slice(g * LANES, (g + 1) * LANES)
        out_ref[gs, out_at : out_at + source.shape[0]] = source[:, gs].T.astype(out_ref.dtype)


def spread_rows(row):
    return jnp.broadcast_to(row, (LANES, LANES)).T


def gather_rows(block):
    return jnp.sum(block.T, axis=0, keepdims=True)


def dual_rows(dual, own_first):
    high, mid, low = (part.astype(F32) for part in split3(dual))
    at = lax.broadcasted_iota(jnp.int32, (8, dual.shape[1]), 0)
    first = 0 if own_first else 3
    ones = jnp.where(at < 6, 1.0, 0.0)
    rows = jnp.where(
        at == first, high, jnp.where(at == first + 1, mid, jnp.where(at == first + 2, low, ones))
    )
    return jnp.concatenate([rows, jnp.zeros((56, dual.shape[1]), F32)], axis=0)


def first_kernel(total, emb_ref, tgt_ref, cen_ref, pd_ref, cd_ref, plan_ref, cot_ref, rows_ref, cols_ref,
                 lhs_ref, tlhs_ref, rhs_ref, rm_ref, rl_ref, cm_ref, cl_ref, pdual_ref, cdual_ref):
    rows, cols = plan_ref.shape
    flat_row(pd_ref[...], pdual_ref)
    flat_row(cd_ref[...] - math.log(total), cdual_ref)
    eh, el = (part.astype(F32) for part in split2(emb_ref[...] * (1.0 / EPSILON)))
    th, tl = (part.astype(F32) for part in split2(tgt_ref[...]))
    transpose_into(lhs_ref, jnp.concatenate([eh, eh], axis=0))
    transpose_into(lhs_ref, jnp.concatenate([el, dual_rows(pdual_ref[...], True)], axis=0), LANES)
    transpose_into(tlhs_ref, jnp.concatenate([th, th], axis=0))
    transpose_into(tlhs_ref, jnp.concatenate([tl, jnp.zeros_like(tl)], axis=0), LANES)
    ch, cl = split2(cen_ref[...])
    rhs_ref[...] = jnp.concatenate([ch, cl, ch, dual_rows(cdual_ref[...], False).astype(BF16)], axis=0)
    cm_ref[...] = jnp.zeros_like(cm_ref)
    cl_ref[...] = jnp.zeros_like(cl_ref)
    tm, tn = 128, 256

    @pl.loop(0, rows // tm)
    def _(i):
        at = pl.ds(pl.multiple_of(i * tm, tm), tm)
        left = lhs_ref[at, :]
        tleft = tlhs_ref[at, :]
        mass = jnp.zeros((tm, LANES), F32)
        load = jnp.zeros((tm, LANES), F32)
        for j in range(cols // tn):
            js = slice(j * tn, (j + 1) * tn)
            right = rhs_ref[:, js]
            plan = jnp.exp(dot(left, right))
            cot = dot(tleft, right)
            plan_ref[at, js] = plan
            cot_ref[at, js] = cot
            weighted = plan * cot
            for h in range(tn // LANES):
                hs = slice(h * LANES, (h + 1) * LANES)
                mass = mass + plan[:, hs]
                load = load + weighted[:, hs]
            cm_ref[:, js] += jnp.sum(plan.reshape(tm // 8, 8, tn), axis=0)
            cl_ref[:, js] += jnp.sum(weighted.reshape(tm // 8, 8, tn), axis=0)
        rm_ref[at, :] = mass
        rl_ref[at, :] = load

    groups = rows // LANES
    for g in range(groups):
        gs = slice(g * LANES, (g + 1) * LANES)
        rows_ref[g : g + 1, :] = gather_rows(rm_ref[gs, :])
        rows_ref[groups + g : groups + g + 1, :] = gather_rows(rl_ref[gs, :])
    tiles = cols // LANES
    for t in range(tiles):
        ts = slice(t * LANES, (t + 1) * LANES)
        cols_ref[t : t + 1, :] = jnp.sum(cm_ref[:, ts], axis=0, keepdims=True)
        cols_ref[tiles + t : tiles + t + 1, :] = jnp.sum(cl_ref[:, ts], axis=0, keepdims=True)


def columns_of(plan_ref, scales, spread_ref, out_ref):
    rows, cols = plan_ref.shape
    tiles = cols // LANES
    count = len(scales)
    for k, scale in enumerate(scales):
        for g in range(rows // LANES):
            spread_ref[k, g * LANES : (g + 1) * LANES, :] = spread_rows(scale[g : g + 1, :])
    wide = 16 // count
    for t0 in range(0, tiles, wide):
        span = min(wide, tiles - t0)

        def step(i, acc, t0=t0, span=span):
            acc = list(acc)
            for r in range(2):
                at = pl.ds(pl.multiple_of(i * 16 + r * 8, 8), 8)
                scale_rows = [spread_ref[k, at, :] for k in range(count)]
                for t in range(span):
                    tile = plan_ref[at, (t0 + t) * LANES : (t0 + t + 1) * LANES]
                    for k in range(count):
                        acc[k * span + t] = acc[k * span + t] + tile * scale_rows[k]
            return tuple(acc)

        zero = jnp.zeros((8, LANES), F32)
        acc = lax.fori_loop(0, rows // 16, step, (zero,) * (count * span))
        for k in range(count):
            for t in range(span):
                at = k * tiles + t0 + t
                out_ref[at : at + 1, :] = jnp.sum(acc[k * span + t], axis=0, keepdims=True)


def rows_of(plan_ref, scales, part_ref, out_ref):
    rows, cols = plan_ref.shape
    tiles = cols // LANES
    groups = rows // LANES
    count = len(scales)
    spread = [
        [jnp.broadcast_to(scale[t : t + 1, :], (8, LANES)) for t in range(tiles)] for scale in scales
    ]

    @pl.loop(0, rows // 16)
    def _(i):
        for r in range(2):
            at = pl.ds(pl.multiple_of(i * 16 + r * 8, 8), 8)
            sums = [[None, None] for _ in range(count)]
            for t in range(tiles):
                tile = plan_ref[at, t * LANES : (t + 1) * LANES]
                for k in range(count):
                    term = tile * spread[k][t]
                    old = sums[k][t % 2]
                    sums[k][t % 2] = term if old is None else old + term
            for k in range(count):
                one, two = sums[k]
                part_ref[k, at, :] = one if two is None else one + two

    for k in range(count):
        for g in range(groups):
            at = k * groups + g
            out_ref[at : at + 1, :] = gather_rows(part_ref[k, g * LANES : (g + 1) * LANES, :])


def second_kernel(plan_ref, rows_ref, cols_ref, out_ref, own_ref, spread_ref):
    groups = rows_ref.shape[0] // 2
    tiles = own_ref.shape[0]
    scale = rows_ref[groups:, :] / rows_ref[:groups, :]
    columns_of(plan_ref, [scale], spread_ref, own_ref)
    out_ref[: 2 * tiles, :] = cols_ref[...]
    out_ref[2 * tiles :, :] = own_ref[...]


def third_kernel(plan_ref, cols_ref, out_ref, part_ref):
    tiles = cols_ref.shape[0] // 3
    mass = cols_ref[:tiles, :]
    load = cols_ref[tiles : 2 * tiles, :]
    beta = load - cols_ref[2 * tiles :, :]
    rows_of(plan_ref, [load / mass, beta / mass], part_ref, out_ref)


def fourth_kernel(plan_ref, rows_ref, terms_ref, out_ref, spread_ref):
    groups = rows_ref.shape[0] // 2
    mass = rows_ref[:groups, :]
    load = rows_ref[groups:, :]
    scales = [(load - terms_ref[k * groups : (k + 1) * groups, :]) / mass for k in range(2)]
    columns_of(plan_ref, scales, spread_ref, out_ref)


def fifth_kernel(plan_ref, cols_ref, terms_ref, out_ref, part_ref):
    tiles = cols_ref.shape[0] // 3
    beta = cols_ref[tiles : 2 * tiles, :] - terms_ref[:tiles, :]
    rows_of(plan_ref, [beta / cols_ref[:tiles, :]], part_ref, out_ref)


def weights_of(plan_ref, cot_ref, spread_ref, low, at, js):
    tn = js.stop - js.start
    spread = spread_ref[at, :]
    tm = spread.shape[0]
    shift = jnp.tile(spread, (1, tn // LANES)).reshape(tm // 8, 8, tn) + low[None]
    return split2(plan_ref[at, js] * (cot_ref[at, js] - shift.reshape(tm, tn)))


def scales_of(rows_ref, aterms_ref, cols_ref, bterms_ref, spread_ref, beta_ref):
    groups = rows_ref.shape[0] // 2
    tiles = cols_ref.shape[0] // 3
    alpha = (rows_ref[groups:, :] - aterms_ref[...]) / rows_ref[:groups, :]
    for g in range(groups):
        spread_ref[g * LANES : (g + 1) * LANES, :] = spread_rows(alpha[g : g + 1, :])
    beta = (cols_ref[tiles : 2 * tiles, :] - bterms_ref[tiles:, :]) / cols_ref[:tiles, :]
    for t in range(tiles):
        beta_ref[:, t * LANES : (t + 1) * LANES] = jnp.broadcast_to(beta[t : t + 1, :], (8, LANES))


def emb_kernel(plan_ref, cot_ref, cen_ref, rows_ref, aterms_ref, cols_ref, bterms_ref,
               keep_ref, send_ref, spread_out_ref, beta_ref, right_ref):
    _, cols = plan_ref.shape
    scales_of(rows_ref, aterms_ref, cols_ref, bterms_ref, spread_out_ref, beta_ref)
    ch, cl = split2(cen_ref[...])
    transpose_into(right_ref, jnp.concatenate([ch.astype(F32), cl.astype(F32)], axis=0))
    tn = 256
    half, width, span = keep_ref.shape
    chunks = 2 * half
    me = lax.axis_index("cen") & (half - 1)
    for q in range(chunks):
        at = pl.ds(pl.multiple_of((me ^ reverse_bits(q, chunks)) * span, span), span)
        acc = jnp.zeros((span, LANES), F32)
        for j in range(cols // tn):
            js = slice(j * tn, (j + 1) * tn)
            wh, wl = weights_of(plan_ref, cot_ref, spread_out_ref, beta_ref[:, js], at, js)
            right = right_ref[js, :]
            acc = acc + dot(wh, right) + dot(wl, right)
        flipped = acc.T
        to_ref = keep_ref if q < half else send_ref
        to_ref[q % half] = flipped[:width] + flipped[width:]


def cen_kernel(plan_ref, cot_ref, emb_ref, spread_ref, beta_ref, gcen_ref):
    rows, cols = plan_ref.shape
    left = jnp.concatenate(split2(emb_ref[...]), axis=0)
    tn = 256
    tm = 256
    chunks, width, chunk_cols = gcen_ref.shape
    me = lax.axis_index("pts")
    for j in range(cols // tn):
        js = slice(j * tn, (j + 1) * tn)
        gcen = jnp.zeros((2 * width, tn), F32)
        for i in range(rows // tm):
            at = slice(i * tm, (i + 1) * tm)
            wh, wl = weights_of(plan_ref, cot_ref, spread_ref, beta_ref[:, js], at, js)
            gcen = gcen + dot(left[:, at], wh) + dot(left[:, at], wl)
        gcen = gcen[:width] + gcen[width:]
        span = min(chunk_cols, tn)
        for s in range(tn // span):
            col = j * tn + s * span
            gcen_ref[reverse_bits(me ^ (col // chunk_cols), chunks), :, pl.ds(col % chunk_cols, span)] = gcen[
                :, s * span : (s + 1) * span
            ]


def last_kernel(gemb_ref, emb_ref):
    chunks, _, span = gemb_ref.shape
    me = lax.axis_index("cen") & (chunks // 2 - 1)
    for q in range(chunks):
        emb_ref[:, q * span : (q + 1) * span] = gemb_ref[reverse_bits(me ^ q, chunks)]


def swap(value, axis, count, bit):
    return lax.ppermute(value, axis, [(i, i ^ bit) for i in range(count)])


def sum_all(value, axis, count):
    for bit in bits_of(count):
        value = value + swap(value, axis, count, bit)
    return value


def shards(embeddings, centroids, point_duals, centroid_duals, targets):
    pts = lax.axis_size("pts")
    cen = lax.axis_size("cen")
    rows, width = embeddings.shape
    cols = centroids.shape[0]
    emb, tgt, ctr = embeddings.T, targets.T, centroids.T
    groups, tiles = rows // LANES, cols // LANES
    sds = jax.ShapeDtypeStruct

    def call(body, outs, scratch, mib, specs, *args, flops=1 << 30):
        return pl.pallas_call(
            body,
            out_shape=outs,
            in_specs=specs,
            out_specs=jax.tree.map(lambda _: VMEM, outs),
            scratch_shapes=scratch,
            cost_estimate=pl.CostEstimate(flops=flops, transcendentals=0, bytes_accessed=1 << 20),
            compiler_params=pltpu.CompilerParams(vmem_limit_bytes=mib << 20),
        )(*args)

    def first(*args):
        return first_kernel(float(cols * cen), *args)

    plan, cot, row_sums, col_sums = call(
        first,
        (
            pltpu.VMEM((rows, cols), F32),
            pltpu.VMEM((rows, cols), F32),
            pltpu.VMEM((2 * groups, LANES), F32),
            pltpu.VMEM((2 * tiles, LANES), F32),
        ),
        [
            pltpu.VMEM((rows, 256), BF16),
            pltpu.VMEM((rows, 256), BF16),
            pltpu.VMEM((256, cols), BF16),
            pltpu.VMEM((rows, LANES), F32),
            pltpu.VMEM((rows, LANES), F32),
            pltpu.VMEM((8, cols), F32),
            pltpu.VMEM((8, cols), F32),
            pltpu.VMEM((1, rows), F32),
            pltpu.VMEM((1, cols), F32),
        ],
        24,
        [VMEM] * 5,
        emb,
        tgt,
        ctr,
        point_duals.reshape(groups, LANES),
        centroid_duals.reshape(tiles, LANES),
    )
    row_sums = sum_all(row_sums, "cen", cen)
    col_all = call(
        second_kernel,
        pltpu.VMEM((3 * tiles, LANES), F32),
        [pltpu.VMEM((tiles, LANES), F32), pltpu.VMEM((1, rows, LANES), F32)],
        6,
        [VMEM] * 3,
        plan,
        row_sums,
        col_sums,
    )
    col_all = sum_all(col_all, "pts", pts)
    row_terms = call(
        third_kernel,
        pltpu.VMEM((2 * groups, LANES), F32),
        [pltpu.VMEM((2, rows, LANES), F32)],
        6,
        [VMEM] * 2,
        plan,
        col_all,
    )
    row_terms = sum_all(row_terms, "cen", cen)
    col_terms = call(
        fourth_kernel,
        pltpu.VMEM((2 * tiles, LANES), F32),
        [pltpu.VMEM((2, rows, LANES), F32)],
        6,
        [VMEM] * 3,
        plan,
        row_sums,
        row_terms,
    )
    col_terms = sum_all(col_terms, "pts", pts)
    last_terms = call(
        fifth_kernel,
        pltpu.VMEM((groups, LANES), F32),
        [pltpu.VMEM((1, rows, LANES), F32)],
        6,
        [VMEM] * 3,
        plan,
        col_all,
        col_terms,
    )
    last_terms = sum_all(last_terms, "cen", cen)
    gemb, sent, spread, beta = call(
        emb_kernel,
        (
            pltpu.VMEM((cen // 2, width, rows // cen), F32),
            pltpu.VMEM((cen // 2, width, rows // cen), F32),
            pltpu.VMEM((rows, LANES), F32),
            pltpu.VMEM((8, cols), F32),
        ),
        [pltpu.VMEM((cols, LANES), BF16)],
        12,
        [VMEM] * 7,
        plan,
        cot,
        ctr,
        row_sums,
        last_terms,
        col_all,
        col_terms,
    )
    sent = swap(sent, "cen", cen, 1)
    gcen = call(
        cen_kernel,
        pltpu.VMEM((pts, width, cols // pts), F32),
        [],
        12,
        [VMEM] * 5,
        plan,
        cot,
        emb,
        spread,
        beta,
        flops=1 << 33,
    )
    cbits, pbits = bits_of(cen), bits_of(pts)
    gemb = gemb + sent
    for bit in cbits[1:-1]:
        keep = gemb.shape[0] // 2
        gemb = gemb[:keep] + swap(gemb[keep:], "cen", cen, bit)
    gemb = gemb + swap(gemb, "cen", cen, cbits[-1])
    for bit in reversed(cbits[:-1]):
        gemb = jnp.concatenate([gemb, swap(gemb, "cen", cen, bit)], axis=0)
    for bit in pbits:
        keep = gcen.shape[0] // 2
        gcen = gcen[:keep] + swap(gcen[keep:], "pts", pts, bit)
    grad_emb = call(last_kernel, sds((width, rows), F32), [], 6, [VMEM], gemb)
    return grad_emb.T, gcen[0].T


def solution(mesh):
    in_specs = (P("pts", None), P("cen", None), P("pts"), P("cen"), P("pts", None))
    out_specs = (P("pts", None), P(("cen", "pts"), None))
    return jax.shard_map(shards, mesh=mesh, in_specs=in_specs, out_specs=out_specs, check_vma=False)
```

```python
import math

import jax
import jax.numpy as jnp
from jax import lax
from jax.experimental import pallas as pl
from jax.experimental.pallas import tpu as pltpu
from jax.sharding import PartitionSpec as P


EPSILON = 0.08
LANES = 128
F32 = jnp.float32
BF16 = jnp.bfloat16
VMEM = pl.BlockSpec(memory_space=pltpu.VMEM)


def bits_of(count):
    return [1 << b for b in range(count.bit_length() - 1)]


def reverse_bits(k, count):
    size = len(bits_of(count))
    return sum(((k >> b) & 1) << (size - 1 - b) for b in range(size))


def split2(x):
    high = x.astype(BF16)
    low = (x - high.astype(F32)).astype(BF16)
    return high, low


def split3(x):
    high = x.astype(BF16)
    rest = x - high.astype(F32)
    mid = rest.astype(BF16)
    low = (rest - mid.astype(F32)).astype(BF16)
    return high, mid, low


def dot(a, b):
    return jnp.dot(a, b, preferred_element_type=F32)


def flat_row(blocks, out_ref):
    for g in range(blocks.shape[0]):
        out_ref[:, g * LANES : (g + 1) * LANES] = blocks[g : g + 1, :]


def transpose_into(out_ref, source, out_at=0):
    for g in range(source.shape[1] // LANES):
        gs = slice(g * LANES, (g + 1) * LANES)
        out_ref[gs, out_at : out_at + source.shape[0]] = source[:, gs].T.astype(out_ref.dtype)


def spread_rows(row):
    return jnp.broadcast_to(row, (LANES, LANES)).T


def gather_rows(block):
    return jnp.sum(block.T, axis=0, keepdims=True)


def dual_rows(dual, own_first):
    high, mid, low = (part.astype(F32) for part in split3(dual))
    at = lax.broadcasted_iota(jnp.int32, (8, dual.shape[1]), 0)
    first = 0 if own_first else 3
    ones = jnp.where(at < 6, 1.0, 0.0)
    rows = jnp.where(
        at == first, high, jnp.where(at == first + 1, mid, jnp.where(at == first + 2, low, ones))
    )
    return jnp.concatenate([rows, jnp.zeros((56, dual.shape[1]), F32)], axis=0)


def first_kernel(total, emb_hbm, tgt_hbm, cen_hbm, pd_hbm, cd_hbm, plan_ref, cot_ref, rows_ref, cols_ref,
                 emb_ref, tgt_ref, cen_ref, pd_ref, cd_ref, sems, lhs_ref, tlhs_ref, rhs_ref, rm_ref, rl_ref, cm_ref, cl_ref, pdual_ref, cdual_ref):
    rows, cols = plan_ref.shape
    copies = [
        pltpu.make_async_copy(source, target, sems.at[k])
        for k, (source, target) in enumerate(
            [(cen_hbm, cen_ref), (cd_hbm, cd_ref), (emb_hbm, emb_ref), (pd_hbm, pd_ref), (tgt_hbm, tgt_ref)]
        )
    ]
    for copy in copies:
        copy.start()
    cm_ref[...] = jnp.zeros_like(cm_ref)
    cl_ref[...] = jnp.zeros_like(cl_ref)
    for copy in copies:
        copy.wait()
    flat_row(pd_ref[...], pdual_ref)
    flat_row(cd_ref[...] - math.log(total), cdual_ref)
    eh, el = (part.astype(F32) for part in split2(emb_ref[...] * (1.0 / EPSILON)))
    th, tl = (part.astype(F32) for part in split2(tgt_ref[...]))
    transpose_into(lhs_ref, jnp.concatenate([eh, eh], axis=0))
    transpose_into(lhs_ref, jnp.concatenate([el, dual_rows(pdual_ref[...], True)], axis=0), LANES)
    transpose_into(tlhs_ref, jnp.concatenate([th, th], axis=0))
    transpose_into(tlhs_ref, jnp.concatenate([tl, jnp.zeros_like(tl)], axis=0), LANES)
    ch, cl = split2(cen_ref[...])
    rhs_ref[...] = jnp.concatenate([ch, cl, ch, dual_rows(cdual_ref[...], False).astype(BF16)], axis=0)
    tm, tn = 128, 256

    @pl.loop(0, rows // tm)
    def _(i):
        at = pl.ds(pl.multiple_of(i * tm, tm), tm)
        left = lhs_ref[at, :]
        tleft = tlhs_ref[at, :]
        mass = jnp.zeros((tm, LANES), F32)
        load = jnp.zeros((tm, LANES), F32)
        for j in range(cols // tn):
            js = slice(j * tn, (j + 1) * tn)
            right = rhs_ref[:, js]
            plan = jnp.exp(dot(left, right))
            cot = dot(tleft, right)
            plan_ref[at, js] = plan
            cot_ref[at, js] = cot
            weighted = plan * cot
            for h in range(tn // LANES):
                hs = slice(h * LANES, (h + 1) * LANES)
                mass = mass + plan[:, hs]
                load = load + weighted[:, hs]
            cm_ref[:, js] += jnp.sum(plan.reshape(tm // 8, 8, tn), axis=0)
            cl_ref[:, js] += jnp.sum(weighted.reshape(tm // 8, 8, tn), axis=0)
        rm_ref[at, :] = mass
        rl_ref[at, :] = load

    groups = rows // LANES
    for g in range(groups):
        gs = slice(g * LANES, (g + 1) * LANES)
        rows_ref[g : g + 1, :] = gather_rows(rm_ref[gs, :])
        rows_ref[groups + g : groups + g + 1, :] = gather_rows(rl_ref[gs, :])
    tiles = cols // LANES
    for t in range(tiles):
        ts = slice(t * LANES, (t + 1) * LANES)
        cols_ref[t : t + 1, :] = jnp.sum(cm_ref[:, ts], axis=0, keepdims=True)
        cols_ref[tiles + t : tiles + t + 1, :] = jnp.sum(cl_ref[:, ts], axis=0, keepdims=True)


def columns_of(plan_ref, scales, spread_ref, out_ref):
    rows, cols = plan_ref.shape
    tiles = cols // LANES
    count = len(scales)
    for k, scale in enumerate(scales):
        for g in range(rows // LANES):
            spread_ref[k, g * LANES : (g + 1) * LANES, :] = spread_rows(scale[g : g + 1, :])
    wide = 16 // count
    for t0 in range(0, tiles, wide):
        span = min(wide, tiles - t0)

        def step(i, acc, t0=t0, span=span):
            acc = list(acc)
            for r in range(2):
                at = pl.ds(pl.multiple_of(i * 16 + r * 8, 8), 8)
                scale_rows = [spread_ref[k, at, :] for k in range(count)]
                for t in range(span):
                    tile = plan_ref[at, (t0 + t) * LANES : (t0 + t + 1) * LANES]
                    for k in range(count):
                        acc[k * span + t] = acc[k * span + t] + tile * scale_rows[k]
            return tuple(acc)

        zero = jnp.zeros((8, LANES), F32)
        acc = lax.fori_loop(0, rows // 16, step, (zero,) * (count * span))
        for k in range(count):
            for t in range(span):
                at = k * tiles + t0 + t
                out_ref[at : at + 1, :] = jnp.sum(acc[k * span + t], axis=0, keepdims=True)


def rows_of(plan_ref, scales, part_ref, out_ref):
    rows, cols = plan_ref.shape
    tiles = cols // LANES
    groups = rows // LANES
    count = len(scales)
    spread = [
        [jnp.broadcast_to(scale[t : t + 1, :], (8, LANES)) for t in range(tiles)] for scale in scales
    ]

    @pl.loop(0, rows // 16)
    def _(i):
        for r in range(2):
            at = pl.ds(pl.multiple_of(i * 16 + r * 8, 8), 8)
            sums = [[None, None] for _ in range(count)]
            for t in range(tiles):
                tile = plan_ref[at, t * LANES : (t + 1) * LANES]
                for k in range(count):
                    term = tile * spread[k][t]
                    old = sums[k][t % 2]
                    sums[k][t % 2] = term if old is None else old + term
            for k in range(count):
                one, two = sums[k]
                part_ref[k, at, :] = one if two is None else one + two

    for k in range(count):
        for g in range(groups):
            at = k * groups + g
            out_ref[at : at + 1, :] = gather_rows(part_ref[k, g * LANES : (g + 1) * LANES, :])


def second_kernel(plan_ref, rows_ref, cols_ref, out_ref, own_ref, spread_ref):
    groups = rows_ref.shape[0] // 2
    tiles = own_ref.shape[0]
    scale = rows_ref[groups:, :] / rows_ref[:groups, :]
    columns_of(plan_ref, [scale], spread_ref, own_ref)
    out_ref[: 2 * tiles, :] = cols_ref[...]
    out_ref[2 * tiles :, :] = own_ref[...]


def third_kernel(plan_ref, cols_ref, out_ref, part_ref):
    tiles = cols_ref.shape[0] // 3
    mass = cols_ref[:tiles, :]
    load = cols_ref[tiles : 2 * tiles, :]
    beta = load - cols_ref[2 * tiles :, :]
    rows_of(plan_ref, [load / mass, beta / mass], part_ref, out_ref)


def fourth_kernel(plan_ref, rows_ref, terms_ref, out_ref, spread_ref):
    groups = rows_ref.shape[0] // 2
    mass = rows_ref[:groups, :]
    load = rows_ref[groups:, :]
    scales = [(load - terms_ref[k * groups : (k + 1) * groups, :]) / mass for k in range(2)]
    columns_of(plan_ref, scales, spread_ref, out_ref)


def fifth_kernel(plan_ref, cols_ref, terms_ref, out_ref, part_ref):
    tiles = cols_ref.shape[0] // 3
    beta = cols_ref[tiles : 2 * tiles, :] - terms_ref[:tiles, :]
    rows_of(plan_ref, [beta / cols_ref[:tiles, :]], part_ref, out_ref)


def weights_of(plan_ref, cot_ref, spread_ref, low, at, js):
    tn = js.stop - js.start
    spread = spread_ref[at, :]
    tm = spread.shape[0]
    shift = jnp.tile(spread, (1, tn // LANES)).reshape(tm // 8, 8, tn) + low[None]
    return split2(plan_ref[at, js] * (cot_ref[at, js] - shift.reshape(tm, tn)))


def scales_of(rows_ref, aterms_ref, cols_ref, bterms_ref, spread_ref, beta_ref):
    groups = rows_ref.shape[0] // 2
    tiles = cols_ref.shape[0] // 3
    alpha = (rows_ref[groups:, :] - aterms_ref[...]) / rows_ref[:groups, :]
    for g in range(groups):
        spread_ref[g * LANES : (g + 1) * LANES, :] = spread_rows(alpha[g : g + 1, :])
    beta = (cols_ref[tiles : 2 * tiles, :] - bterms_ref[tiles:, :]) / cols_ref[:tiles, :]
    for t in range(tiles):
        beta_ref[:, t * LANES : (t + 1) * LANES] = jnp.broadcast_to(beta[t : t + 1, :], (8, LANES))


def emb_kernel(plan_ref, cot_ref, cen_ref, rows_ref, aterms_ref, cols_ref, bterms_ref,
               keep_ref, send_ref, spread_out_ref, beta_ref, right_ref):
    _, cols = plan_ref.shape
    scales_of(rows_ref, aterms_ref, cols_ref, bterms_ref, spread_out_ref, beta_ref)
    ch, cl = split2(cen_ref[...])
    transpose_into(right_ref, jnp.concatenate([ch.astype(F32), cl.astype(F32)], axis=0))
    tn = 256
    half, width, span = keep_ref.shape
    chunks = 2 * half
    me = lax.axis_index("cen") & (half - 1)
    for q in range(chunks):
        at = pl.ds(pl.multiple_of((me ^ reverse_bits(q, chunks)) * span, span), span)
        acc = jnp.zeros((span, LANES), F32)
        for j in range(cols // tn):
            js = slice(j * tn, (j + 1) * tn)
            wh, wl = weights_of(plan_ref, cot_ref, spread_out_ref, beta_ref[:, js], at, js)
            right = right_ref[js, :]
            acc = acc + dot(wh, right) + dot(wl, right)
        flipped = acc.T
        to_ref = keep_ref if q < half else send_ref
        to_ref[q % half] = flipped[:width] + flipped[width:]


def cen_kernel(plan_ref, cot_ref, emb_ref, spread_ref, beta_ref, gcen_ref):
    rows, cols = plan_ref.shape
    left = jnp.concatenate(split2(emb_ref[...]), axis=0)
    tn = 256
    tm = 256
    chunks, width, chunk_cols = gcen_ref.shape
    me = lax.axis_index("pts")
    for j in range(cols // tn):
        js = slice(j * tn, (j + 1) * tn)
        gcen = jnp.zeros((2 * width, tn), F32)
        for i in range(rows // tm):
            at = slice(i * tm, (i + 1) * tm)
            wh, wl = weights_of(plan_ref, cot_ref, spread_ref, beta_ref[:, js], at, js)
            gcen = gcen + dot(left[:, at], wh) + dot(left[:, at], wl)
        gcen = gcen[:width] + gcen[width:]
        span = min(chunk_cols, tn)
        for s in range(tn // span):
            col = j * tn + s * span
            gcen_ref[reverse_bits(me ^ (col // chunk_cols), chunks), :, pl.ds(col % chunk_cols, span)] = gcen[
                :, s * span : (s + 1) * span
            ]


def last_kernel(own_ref, got_ref, mine_ref, theirs_ref, emb_ref, cen_ref):
    half, _, span = own_ref.shape
    chunks = 2 * half
    me = lax.axis_index("cen") & (half - 1)
    for q in range(chunks):
        place = me ^ reverse_bits(q, chunks)
        at = pl.ds(pl.multiple_of(place * span, span), span)
        from_ref = own_ref if q < half else got_ref
        emb_ref[:, at] = from_ref[q % half]
    cen_ref[...] = mine_ref[...] + theirs_ref[...]


def swap(value, axis, count, bit):
    return lax.ppermute(value, axis, [(i, i ^ bit) for i in range(count)])


def sum_all(value, axis, count, first):
    bits = bits_of(count)
    groups = [bits[:first]] + [bits[at : at + 2] for at in range(first, len(bits), 2)]
    for group in groups:
        if len(group) == 1:
            value = value + swap(value, axis, count, group[0])
        else:
            one, two = group
            near = swap(value, axis, count, one)
            far = swap(value, axis, count, two)
            both = swap(value, axis, count, one + two)
            value = (value + near) + (far + both)
    return value


def shards(embeddings, centroids, point_duals, centroid_duals, targets):
    pts = lax.axis_size("pts")
    cen = lax.axis_size("cen")
    rows, width = embeddings.shape
    cols = centroids.shape[0]
    emb, tgt, ctr = embeddings.T, targets.T, centroids.T
    groups, tiles = rows // LANES, cols // LANES
    sds = jax.ShapeDtypeStruct

    def call(body, outs, scratch, mib, specs, *args, flops=1 << 30):
        return pl.pallas_call(
            body,
            out_shape=outs,
            in_specs=specs,
            out_specs=jax.tree.map(lambda _: VMEM, outs),
            scratch_shapes=scratch,
            cost_estimate=pl.CostEstimate(flops=flops, transcendentals=0, bytes_accessed=1 << 20),
            compiler_params=pltpu.CompilerParams(vmem_limit_bytes=mib << 20),
        )(*args)

    def first(*args):
        return first_kernel(float(cols * cen), *args)

    plan, cot, row_sums, col_sums = call(
        first,
        (
            pltpu.VMEM((rows, cols), F32),
            pltpu.VMEM((rows, cols), F32),
            pltpu.VMEM((2 * groups, LANES), F32),
            pltpu.VMEM((2 * tiles, LANES), F32),
        ),
        [
            pltpu.VMEM((width, rows), F32),
            pltpu.VMEM((width, rows), F32),
            pltpu.VMEM((width, cols), F32),
            pltpu.VMEM((groups, LANES), F32),
            pltpu.VMEM((tiles, LANES), F32),
            pltpu.SemaphoreType.DMA((5,)),
            pltpu.VMEM((rows, 256), BF16),
            pltpu.VMEM((rows, 256), BF16),
            pltpu.VMEM((256, cols), BF16),
            pltpu.VMEM((rows, LANES), F32),
            pltpu.VMEM((rows, LANES), F32),
            pltpu.VMEM((8, cols), F32),
            pltpu.VMEM((8, cols), F32),
            pltpu.VMEM((1, rows), F32),
            pltpu.VMEM((1, cols), F32),
        ],
        24,
        [pl.BlockSpec(memory_space=pltpu.HBM)] * 5,
        emb,
        tgt,
        ctr,
        point_duals.reshape(groups, LANES),
        centroid_duals.reshape(tiles, LANES),
    )
    row_sums = sum_all(row_sums, "cen", cen, 2)
    col_all = call(
        second_kernel,
        pltpu.VMEM((3 * tiles, LANES), F32),
        [pltpu.VMEM((tiles, LANES), F32), pltpu.VMEM((1, rows, LANES), F32)],
        6,
        [VMEM] * 3,
        plan,
        row_sums,
        col_sums,
    )
    col_all = sum_all(col_all, "pts", pts, 1)
    row_terms = call(
        third_kernel,
        pltpu.VMEM((2 * groups, LANES), F32),
        [pltpu.VMEM((2, rows, LANES), F32)],
        6,
        [VMEM] * 2,
        plan,
        col_all,
    )
    row_terms = sum_all(row_terms, "cen", cen, 2)
    col_terms = call(
        fourth_kernel,
        pltpu.VMEM((2 * tiles, LANES), F32),
        [pltpu.VMEM((2, rows, LANES), F32)],
        6,
        [VMEM] * 3,
        plan,
        row_sums,
        row_terms,
    )
    col_terms = sum_all(col_terms, "pts", pts, 1)
    last_terms = call(
        fifth_kernel,
        pltpu.VMEM((groups, LANES), F32),
        [pltpu.VMEM((1, rows, LANES), F32)],
        6,
        [VMEM] * 3,
        plan,
        col_all,
        col_terms,
    )
    last_terms = sum_all(last_terms, "cen", cen, 2)
    gemb, sent, spread, beta = call(
        emb_kernel,
        (
            pltpu.VMEM((cen // 2, width, rows // cen), F32),
            pltpu.VMEM((cen // 2, width, rows // cen), F32),
            pltpu.VMEM((rows, LANES), F32),
            pltpu.VMEM((8, cols), F32),
        ),
        [pltpu.VMEM((cols, LANES), BF16)],
        12,
        [VMEM] * 7,
        plan,
        cot,
        ctr,
        row_sums,
        last_terms,
        col_all,
        col_terms,
    )
    sent = swap(sent, "cen", cen, 1)
    gcen = call(
        cen_kernel,
        pltpu.VMEM((pts, width, cols // pts), F32),
        [],
        12,
        [VMEM] * 5,
        plan,
        cot,
        emb,
        spread,
        beta,
        flops=1 << 33,
    )
    cbits, pbits = bits_of(cen), bits_of(pts)
    gemb = gemb + sent
    for bit in cbits[1:-1]:
        keep = gemb.shape[0] // 2
        gemb = gemb[:keep] + swap(gemb[keep:], "cen", cen, bit)
    gemb = gemb + swap(gemb, "cen", cen, cbits[-1])
    for bit in reversed(cbits[1:-1]):
        gemb = jnp.concatenate([gemb, swap(gemb, "cen", cen, bit)], axis=0)
    got = swap(gemb, "cen", cen, cbits[0])
    for bit in pbits[:-1]:
        keep = gcen.shape[0] // 2
        gcen = gcen[:keep] + swap(gcen[keep:], "pts", pts, bit)
    theirs = swap(gcen[1], "pts", pts, pbits[-1])
    grad_emb, grad_cen = call(
        last_kernel,
        (sds((width, rows), F32), sds((width, cols // pts), F32)),
        [],
        6,
        [VMEM] * 4,
        gemb,
        got,
        gcen[0],
        theirs,
    )
    return grad_emb.T, grad_cen.T


def solution(mesh):
    in_specs = (P("pts", None), P("cen", None), P("pts"), P("cen"), P("pts", None))
    out_specs = (P("pts", None), P(("cen", "pts"), None))
    return jax.shard_map(shards, mesh=mesh, in_specs=in_specs, out_specs=out_specs, check_vma=False)
```

```python
import math

import jax
import jax.numpy as jnp
from jax import lax
from jax.experimental import pallas as pl
from jax.experimental.pallas import tpu as pltpu
from jax.sharding import PartitionSpec as P


EPSILON = 0.08
LANES = 128
F32 = jnp.float32
BF16 = jnp.bfloat16
VMEM = pl.BlockSpec(memory_space=pltpu.VMEM)


def bits_of(count):
    return [1 << b for b in range(count.bit_length() - 1)]


def reverse_bits(k, count):
    size = len(bits_of(count))
    return sum(((k >> b) & 1) << (size - 1 - b) for b in range(size))


def split2(x):
    high = x.astype(BF16)
    low = (x - high.astype(F32)).astype(BF16)
    return high, low


def split3(x):
    high = x.astype(BF16)
    rest = x - high.astype(F32)
    mid = rest.astype(BF16)
    low = (rest - mid.astype(F32)).astype(BF16)
    return high, mid, low


def dot(a, b):
    return jnp.dot(a, b, preferred_element_type=F32)


def flat_row(blocks, out_ref):
    for g in range(blocks.shape[0]):
        out_ref[:, g * LANES : (g + 1) * LANES] = blocks[g : g + 1, :]


def transpose_into(out_ref, source, out_at=0):
    for g in range(source.shape[1] // LANES):
        gs = slice(g * LANES, (g + 1) * LANES)
        out_ref[gs, out_at : out_at + source.shape[0]] = source[:, gs].T.astype(out_ref.dtype)


def spread_rows(row):
    return jnp.broadcast_to(row, (LANES, LANES)).T


def gather_rows(block):
    return jnp.sum(block.T, axis=0, keepdims=True)


def dual_rows(dual, own_first):
    high, mid, low = (part.astype(F32) for part in split3(dual))
    at = lax.broadcasted_iota(jnp.int32, (8, dual.shape[1]), 0)
    first = 0 if own_first else 3
    ones = jnp.where(at < 6, 1.0, 0.0)
    rows = jnp.where(
        at == first, high, jnp.where(at == first + 1, mid, jnp.where(at == first + 2, low, ones))
    )
    return jnp.concatenate([rows, jnp.zeros((56, dual.shape[1]), F32)], axis=0)


def first_kernel(total, emb_hbm, tgt_hbm, cen_hbm, pd_hbm, cd_hbm, plan_ref, cot_ref, rows_ref, cols_ref,
                 emb_ref, tgt_ref, cen_ref, pd_ref, cd_ref, sems, lhs_ref, tlhs_ref, rhs_ref, rm_ref, rl_ref, cm_ref, cl_ref, pdual_ref, cdual_ref):
    rows, cols = plan_ref.shape
    copies = [
        pltpu.make_async_copy(source, target, sems.at[k])
        for k, (source, target) in enumerate(
            [(cen_hbm, cen_ref), (cd_hbm, cd_ref), (emb_hbm, emb_ref), (pd_hbm, pd_ref), (tgt_hbm, tgt_ref)]
        )
    ]
    for copy in copies:
        copy.start()
    cm_ref[...] = jnp.zeros_like(cm_ref)
    cl_ref[...] = jnp.zeros_like(cl_ref)
    for copy in copies:
        copy.wait()
    flat_row(pd_ref[...], pdual_ref)
    flat_row(cd_ref[...] - math.log(total), cdual_ref)
    eh, el = (part.astype(F32) for part in split2(emb_ref[...] * (1.0 / EPSILON)))
    th, tl = (part.astype(F32) for part in split2(tgt_ref[...]))
    transpose_into(lhs_ref, jnp.concatenate([eh, eh], axis=0))
    transpose_into(lhs_ref, jnp.concatenate([el, dual_rows(pdual_ref[...], True)], axis=0), LANES)
    transpose_into(tlhs_ref, jnp.concatenate([th, th], axis=0))
    transpose_into(tlhs_ref, jnp.concatenate([tl, jnp.zeros_like(tl)], axis=0), LANES)
    ch, cl = split2(cen_ref[...])
    rhs_ref[...] = jnp.concatenate([ch, cl, ch, dual_rows(cdual_ref[...], False).astype(BF16)], axis=0)
    tm, tn = 128, 256

    @pl.loop(0, rows // tm)
    def _(i):
        at = pl.ds(pl.multiple_of(i * tm, tm), tm)
        left = lhs_ref[at, :]
        tleft = tlhs_ref[at, :]
        mass = jnp.zeros((tm, LANES), F32)
        load = jnp.zeros((tm, LANES), F32)
        for j in range(cols // tn):
            js = slice(j * tn, (j + 1) * tn)
            right = rhs_ref[:, js]
            plan = jnp.exp(dot(left, right))
            cot = dot(tleft, right)
            plan_ref[at, js] = plan
            cot_ref[at, js] = cot
            weighted = plan * cot
            for h in range(tn // LANES):
                hs = slice(h * LANES, (h + 1) * LANES)
                mass = mass + plan[:, hs]
                load = load + weighted[:, hs]
            cm_ref[:, js] += jnp.sum(plan.reshape(tm // 8, 8, tn), axis=0)
            cl_ref[:, js] += jnp.sum(weighted.reshape(tm // 8, 8, tn), axis=0)
        rm_ref[at, :] = mass
        rl_ref[at, :] = load

    groups = rows // LANES
    for g in range(groups):
        gs = slice(g * LANES, (g + 1) * LANES)
        rows_ref[g : g + 1, :] = gather_rows(rm_ref[gs, :])
        rows_ref[groups + g : groups + g + 1, :] = gather_rows(rl_ref[gs, :])
    tiles = cols // LANES
    for t in range(tiles):
        ts = slice(t * LANES, (t + 1) * LANES)
        cols_ref[t : t + 1, :] = jnp.sum(cm_ref[:, ts], axis=0, keepdims=True)
        cols_ref[tiles + t : tiles + t + 1, :] = jnp.sum(cl_ref[:, ts], axis=0, keepdims=True)


def columns_of(plan_ref, scales, spread_ref, out_ref):
    rows, cols = plan_ref.shape
    tiles = cols // LANES
    count = len(scales)
    for k, scale in enumerate(scales):
        for g in range(rows // LANES):
            spread_ref[k, g * LANES : (g + 1) * LANES, :] = spread_rows(scale[g : g + 1, :])
    wide = 16 // count
    for t0 in range(0, tiles, wide):
        span = min(wide, tiles - t0)

        def step(i, acc, t0=t0, span=span):
            acc = list(acc)
            for r in range(2):
                at = pl.ds(pl.multiple_of(i * 16 + r * 8, 8), 8)
                scale_rows = [spread_ref[k, at, :] for k in range(count)]
                for t in range(span):
                    tile = plan_ref[at, (t0 + t) * LANES : (t0 + t + 1) * LANES]
                    for k in range(count):
                        acc[k * span + t] = acc[k * span + t] + tile * scale_rows[k]
            return tuple(acc)

        zero = jnp.zeros((8, LANES), F32)
        acc = lax.fori_loop(0, rows // 16, step, (zero,) * (count * span))
        for k in range(count):
            for t in range(span):
                at = k * tiles + t0 + t
                out_ref[at : at + 1, :] = jnp.sum(acc[k * span + t], axis=0, keepdims=True)


def rows_of(plan_ref, scales, part_ref, out_ref):
    rows, cols = plan_ref.shape
    tiles = cols // LANES
    groups = rows // LANES
    count = len(scales)
    spread = [
        [jnp.broadcast_to(scale[t : t + 1, :], (8, LANES)) for t in range(tiles)] for scale in scales
    ]

    @pl.loop(0, rows // 16)
    def _(i):
        for r in range(2):
            at = pl.ds(pl.multiple_of(i * 16 + r * 8, 8), 8)
            sums = [[None, None] for _ in range(count)]
            for t in range(tiles):
                tile = plan_ref[at, t * LANES : (t + 1) * LANES]
                for k in range(count):
                    term = tile * spread[k][t]
                    old = sums[k][t % 2]
                    sums[k][t % 2] = term if old is None else old + term
            for k in range(count):
                one, two = sums[k]
                part_ref[k, at, :] = one if two is None else one + two

    for k in range(count):
        for g in range(groups):
            at = k * groups + g
            out_ref[at : at + 1, :] = gather_rows(part_ref[k, g * LANES : (g + 1) * LANES, :])


def second_kernel(plan_ref, rows_ref, cols_ref, out_ref, own_ref, spread_ref):
    groups = rows_ref.shape[0] // 2
    tiles = own_ref.shape[0]
    scale = rows_ref[groups:, :] / rows_ref[:groups, :]
    columns_of(plan_ref, [scale], spread_ref, own_ref)
    out_ref[: 2 * tiles, :] = cols_ref[...]
    out_ref[2 * tiles :, :] = own_ref[...]


def third_kernel(plan_ref, cols_ref, out_ref, part_ref):
    tiles = cols_ref.shape[0] // 3
    mass = cols_ref[:tiles, :]
    load = cols_ref[tiles : 2 * tiles, :]
    beta = load - cols_ref[2 * tiles :, :]
    rows_of(plan_ref, [load / mass, beta / mass], part_ref, out_ref)


def fourth_kernel(plan_ref, rows_ref, terms_ref, out_ref, spread_ref):
    groups = rows_ref.shape[0] // 2
    mass = rows_ref[:groups, :]
    load = rows_ref[groups:, :]
    scales = [(load - terms_ref[k * groups : (k + 1) * groups, :]) / mass for k in range(2)]
    columns_of(plan_ref, scales, spread_ref, out_ref)


def fifth_kernel(plan_ref, cols_ref, terms_ref, out_ref, part_ref):
    tiles = cols_ref.shape[0] // 3
    beta = cols_ref[tiles : 2 * tiles, :] - terms_ref[:tiles, :]
    rows_of(plan_ref, [beta / cols_ref[:tiles, :]], part_ref, out_ref)


def weights_of(plan_ref, cot_ref, spread_ref, low, at, js):
    tn = js.stop - js.start
    spread = spread_ref[at, :]
    tm = spread.shape[0]
    shift = jnp.tile(spread, (1, tn // LANES)).reshape(tm // 8, 8, tn) + low[None]
    return split2(plan_ref[at, js] * (cot_ref[at, js] - shift.reshape(tm, tn)))


def scales_of(rows_ref, aterms_ref, cols_ref, bterms_ref, spread_ref, beta_ref):
    groups = rows_ref.shape[0] // 2
    tiles = cols_ref.shape[0] // 3
    alpha = (rows_ref[groups:, :] - aterms_ref[...]) / rows_ref[:groups, :]
    for g in range(groups):
        spread_ref[g * LANES : (g + 1) * LANES, :] = spread_rows(alpha[g : g + 1, :])
    beta = (cols_ref[tiles : 2 * tiles, :] - bterms_ref[tiles:, :]) / cols_ref[:tiles, :]
    for t in range(tiles):
        beta_ref[:, t * LANES : (t + 1) * LANES] = jnp.broadcast_to(beta[t : t + 1, :], (8, LANES))


def emb_kernel(plan_ref, cot_ref, cen_ref, rows_ref, aterms_ref, cols_ref, bterms_ref,
               keep_ref, send_ref, spread_out_ref, beta_ref, right_ref):
    _, cols = plan_ref.shape
    scales_of(rows_ref, aterms_ref, cols_ref, bterms_ref, spread_out_ref, beta_ref)
    ch, cl = split2(cen_ref[...])
    transpose_into(right_ref, jnp.concatenate([ch.astype(F32), cl.astype(F32)], axis=0))
    tn = 256
    half, width, span = keep_ref.shape
    chunks = 2 * half
    me = lax.axis_index("cen") & (half - 1)
    for q in range(chunks):
        at = pl.ds(pl.multiple_of((me ^ reverse_bits(q, chunks)) * span, span), span)
        acc = jnp.zeros((span, LANES), F32)
        for j in range(cols // tn):
            js = slice(j * tn, (j + 1) * tn)
            wh, wl = weights_of(plan_ref, cot_ref, spread_out_ref, beta_ref[:, js], at, js)
            right = right_ref[js, :]
            acc = acc + dot(wh, right) + dot(wl, right)
        flipped = acc.T
        to_ref = keep_ref if q < half else send_ref
        to_ref[q % half] = flipped[:width] + flipped[width:]


def cen_kernel(plan_ref, cot_ref, emb_ref, spread_ref, beta_ref, gcen_ref):
    rows, cols = plan_ref.shape
    left = jnp.concatenate(split2(emb_ref[...]), axis=0)
    tn = 256
    tm = 256
    chunks, width, chunk_cols = gcen_ref.shape
    me = lax.axis_index("pts")
    for j in range(cols // tn):
        js = slice(j * tn, (j + 1) * tn)
        gcen = jnp.zeros((2 * width, tn), F32)
        for i in range(rows // tm):
            at = slice(i * tm, (i + 1) * tm)
            wh, wl = weights_of(plan_ref, cot_ref, spread_ref, beta_ref[:, js], at, js)
            gcen = gcen + dot(left[:, at], wh) + dot(left[:, at], wl)
        gcen = gcen[:width] + gcen[width:]
        span = min(chunk_cols, tn)
        for s in range(tn // span):
            col = j * tn + s * span
            gcen_ref[reverse_bits(me ^ (col // chunk_cols), chunks), :, pl.ds(col % chunk_cols, span)] = gcen[
                :, s * span : (s + 1) * span
            ]


def last_kernel(own_ref, got_ref, mine_ref, theirs_ref, emb_ref, cen_ref):
    half, _, span = own_ref.shape
    chunks = 2 * half
    me = lax.axis_index("cen") & (half - 1)
    for q in range(chunks):
        place = me ^ reverse_bits(q, chunks)
        at = pl.ds(pl.multiple_of(place * span, span), span)
        from_ref = own_ref if q < half else got_ref
        emb_ref[:, at] = from_ref[q % half]
    cen_ref[...] = mine_ref[...] + theirs_ref[...]


def swap(value, axis, count, bit):
    return lax.ppermute(value, axis, [(i, i ^ bit) for i in range(count)])


def sum_all(value, axis, count, first):
    bits = bits_of(count)
    groups = [bits[:first]] + [bits[at : at + 2] for at in range(first, len(bits), 2)]
    for group in groups:
        if len(group) == 1:
            value = value + swap(value, axis, count, group[0])
        else:
            one, two = group
            near = swap(value, axis, count, one)
            far = swap(value, axis, count, two)
            both = swap(value, axis, count, one + two)
            value = (value + near) + (far + both)
    return value


def shards(embeddings, centroids, point_duals, centroid_duals, targets):
    pts = lax.axis_size("pts")
    cen = lax.axis_size("cen")
    rows, width = embeddings.shape
    cols = centroids.shape[0]
    emb, tgt, ctr = embeddings.T, targets.T, centroids.T
    groups, tiles = rows // LANES, cols // LANES
    sds = jax.ShapeDtypeStruct

    def call(body, outs, scratch, mib, specs, *args, flops=1 << 30):
        return pl.pallas_call(
            body,
            out_shape=outs,
            in_specs=specs,
            out_specs=jax.tree.map(lambda _: VMEM, outs),
            scratch_shapes=scratch,
            cost_estimate=pl.CostEstimate(flops=flops, transcendentals=0, bytes_accessed=1 << 20),
            compiler_params=pltpu.CompilerParams(vmem_limit_bytes=mib << 20),
        )(*args)

    def first(*args):
        return first_kernel(float(cols * cen), *args)

    plan, cot, row_sums, col_sums = call(
        first,
        (
            pltpu.VMEM((rows, cols), F32),
            pltpu.VMEM((rows, cols), F32),
            pltpu.VMEM((2 * groups, LANES), F32),
            pltpu.VMEM((2 * tiles, LANES), F32),
        ),
        [
            pltpu.VMEM((width, rows), F32),
            pltpu.VMEM((width, rows), F32),
            pltpu.VMEM((width, cols), F32),
            pltpu.VMEM((groups, LANES), F32),
            pltpu.VMEM((tiles, LANES), F32),
            pltpu.SemaphoreType.DMA((5,)),
            pltpu.VMEM((rows, 256), BF16),
            pltpu.VMEM((rows, 256), BF16),
            pltpu.VMEM((256, cols), BF16),
            pltpu.VMEM((rows, LANES), F32),
            pltpu.VMEM((rows, LANES), F32),
            pltpu.VMEM((8, cols), F32),
            pltpu.VMEM((8, cols), F32),
            pltpu.VMEM((1, rows), F32),
            pltpu.VMEM((1, cols), F32),
        ],
        24,
        [pl.BlockSpec(memory_space=pltpu.HBM)] * 5,
        *(
            pltpu.with_memory_space_constraint(x, pltpu.HBM)
            for x in (emb, tgt, ctr, point_duals.reshape(groups, LANES), centroid_duals.reshape(tiles, LANES))
        ),
    )
    row_sums = sum_all(row_sums, "cen", cen, 2)
    col_all = call(
        second_kernel,
        pltpu.VMEM((3 * tiles, LANES), F32),
        [pltpu.VMEM((tiles, LANES), F32), pltpu.VMEM((1, rows, LANES), F32)],
        6,
        [VMEM] * 3,
        plan,
        row_sums,
        col_sums,
    )
    col_all = sum_all(col_all, "pts", pts, 1)
    row_terms = call(
        third_kernel,
        pltpu.VMEM((2 * groups, LANES), F32),
        [pltpu.VMEM((2, rows, LANES), F32)],
        6,
        [VMEM] * 2,
        plan,
        col_all,
    )
    row_terms = sum_all(row_terms, "cen", cen, 2)
    col_terms = call(
        fourth_kernel,
        pltpu.VMEM((2 * tiles, LANES), F32),
        [pltpu.VMEM((2, rows, LANES), F32)],
        6,
        [VMEM] * 3,
        plan,
        row_sums,
        row_terms,
    )
    col_terms = sum_all(col_terms, "pts", pts, 1)
    last_terms = call(
        fifth_kernel,
        pltpu.VMEM((groups, LANES), F32),
        [pltpu.VMEM((1, rows, LANES), F32)],
        6,
        [VMEM] * 3,
        plan,
        col_all,
        col_terms,
    )
    last_terms = sum_all(last_terms, "cen", cen, 2)
    gemb, sent, spread, beta = call(
        emb_kernel,
        (
            pltpu.VMEM((cen // 2, width, rows // cen), F32),
            pltpu.VMEM((cen // 2, width, rows // cen), F32),
            pltpu.VMEM((rows, LANES), F32),
            pltpu.VMEM((8, cols), F32),
        ),
        [pltpu.VMEM((cols, LANES), BF16)],
        12,
        [VMEM] * 7,
        plan,
        cot,
        ctr,
        row_sums,
        last_terms,
        col_all,
        col_terms,
    )
    sent = swap(sent, "cen", cen, 1)
    gcen = call(
        cen_kernel,
        pltpu.VMEM((pts, width, cols // pts), F32),
        [],
        12,
        [VMEM] * 5,
        plan,
        cot,
        emb,
        spread,
        beta,
        flops=1 << 33,
    )
    cbits, pbits = bits_of(cen), bits_of(pts)
    gemb = gemb + sent
    for bit in cbits[1:-1]:
        keep = gemb.shape[0] // 2
        gemb = gemb[:keep] + swap(gemb[keep:], "cen", cen, bit)
    gemb = gemb + swap(gemb, "cen", cen, cbits[-1])
    for bit in reversed(cbits[1:-1]):
        gemb = jnp.concatenate([gemb, swap(gemb, "cen", cen, bit)], axis=0)
    got = swap(gemb, "cen", cen, cbits[0])
    for bit in pbits[:-1]:
        keep = gcen.shape[0] // 2
        gcen = gcen[:keep] + swap(gcen[keep:], "pts", pts, bit)
    theirs = swap(gcen[1], "pts", pts, pbits[-1])
    grad_emb, grad_cen = call(
        last_kernel,
        (sds((width, rows), F32), sds((width, cols // pts), F32)),
        [],
        6,
        [VMEM] * 4,
        gemb,
        got,
        gcen[0],
        theirs,
    )
    return grad_emb.T, grad_cen.T


def solution(mesh):
    in_specs = (P("pts", None), P("cen", None), P("pts"), P("cen"), P("pts", None))
    out_specs = (P("pts", None), P(("cen", "pts"), None))
    return jax.shard_map(shards, mesh=mesh, in_specs=in_specs, out_specs=out_specs, check_vma=False)
```

```python
import math

import jax
import jax.numpy as jnp
from jax import lax
from jax.experimental import pallas as pl
from jax.experimental.pallas import tpu as pltpu
from jax.sharding import PartitionSpec as P


EPSILON = 0.08
LANES = 128
LOG2_E = math.log2(math.e)
F32 = jnp.float32
BF16 = jnp.bfloat16
VMEM = pl.BlockSpec(memory_space=pltpu.VMEM)


def bits_of(count):
    return [1 << b for b in range(count.bit_length() - 1)]


def reverse_bits(k, count):
    size = len(bits_of(count))
    return sum(((k >> b) & 1) << (size - 1 - b) for b in range(size))


def split2(x):
    high = x.astype(BF16)
    low = (x - high.astype(F32)).astype(BF16)
    return high, low


def split3(x):
    high = x.astype(BF16)
    rest = x - high.astype(F32)
    mid = rest.astype(BF16)
    low = (rest - mid.astype(F32)).astype(BF16)
    return high, mid, low


def dot(a, b):
    return jnp.dot(a, b, preferred_element_type=F32)


def flat_row(blocks, out_ref):
    for g in range(blocks.shape[0]):
        out_ref[:, g * LANES : (g + 1) * LANES] = blocks[g : g + 1, :]


def transpose_into(out_ref, source, out_at=0):
    for g in range(source.shape[1] // LANES):
        gs = slice(g * LANES, (g + 1) * LANES)
        out_ref[gs, out_at : out_at + source.shape[0]] = source[:, gs].T.astype(out_ref.dtype)


def spread_rows(row):
    return jnp.broadcast_to(row, (LANES, LANES)).T


def gather_rows(block):
    return jnp.sum(block.T, axis=0, keepdims=True)


def dual_rows(dual, own_first):
    high, mid, low = (part.astype(F32) for part in split3(dual))
    at = lax.broadcasted_iota(jnp.int32, (8, dual.shape[1]), 0)
    first = 0 if own_first else 3
    ones = jnp.where(at < 6, 1.0, 0.0)
    rows = jnp.where(
        at == first, high, jnp.where(at == first + 1, mid, jnp.where(at == first + 2, low, ones))
    )
    return jnp.concatenate([rows, jnp.zeros((56, dual.shape[1]), F32)], axis=0)


def first_kernel(total, emb_hbm, tgt_hbm, cen_hbm, pd_hbm, cd_hbm, plan_ref, cot_ref, rows_ref, cols_ref,
                 emb_ref, tgt_ref, cen_ref, pd_ref, cd_ref, sems, lhs_ref, rhs_ref, rm_ref, rl_ref, cm_ref, cl_ref, pdual_ref, cdual_ref):
    rows, cols = plan_ref.shape
    copies = [
        pltpu.make_async_copy(source, target, sems.at[k])
        for k, (source, target) in enumerate(
            [(cen_hbm, cen_ref), (cd_hbm, cd_ref), (emb_hbm, emb_ref), (pd_hbm, pd_ref), (tgt_hbm, tgt_ref)]
        )
    ]
    for copy in copies:
        copy.start()
    cm_ref[...] = jnp.zeros_like(cm_ref)
    cl_ref[...] = jnp.zeros_like(cl_ref)
    for copy in copies:
        copy.wait()
    flat_row(pd_ref[...] * LOG2_E, pdual_ref)
    flat_row(cd_ref[...] * LOG2_E - math.log2(total), cdual_ref)
    eh, el = (part.astype(F32) for part in split2(emb_ref[...] * (LOG2_E / EPSILON)))
    th, tl = (part.astype(F32) for part in split2(tgt_ref[...]))
    transpose_into(lhs_ref.at[0], jnp.concatenate([eh, eh], axis=0))
    transpose_into(lhs_ref.at[0], jnp.concatenate([el, dual_rows(pdual_ref[...], True)], axis=0), LANES)
    transpose_into(lhs_ref.at[1], jnp.concatenate([th, th], axis=0))
    transpose_into(lhs_ref.at[1], jnp.concatenate([tl, jnp.zeros_like(tl)], axis=0), LANES)
    ch, cl = split2(cen_ref[...])
    rhs_ref[...] = jnp.concatenate([ch, cl, ch, dual_rows(cdual_ref[...], False).astype(BF16)], axis=0)
    tm, tn = 128, 256

    @pl.loop(0, rows // tm)
    def _(i):
        at = pl.ds(pl.multiple_of(i * tm, tm), tm)
        left = lhs_ref[:, at, :].reshape(2 * tm, 2 * LANES)
        mass = jnp.zeros((tm, LANES), F32)
        load = jnp.zeros((tm, LANES), F32)
        for j in range(cols // tn):
            js = slice(j * tn, (j + 1) * tn)
            right = rhs_ref[:, js]
            both = dot(left, right)
            plan = jnp.exp2(both[:tm])
            cot = both[tm:]
            plan_ref[at, js] = plan
            cot_ref[at, js] = cot
            weighted = plan * cot
            for h in range(tn // LANES):
                hs = slice(h * LANES, (h + 1) * LANES)
                mass = mass + plan[:, hs]
                load = load + weighted[:, hs]
            cm_ref[:, js] += jnp.sum(plan.reshape(tm // 8, 8, tn), axis=0)
            cl_ref[:, js] += jnp.sum(weighted.reshape(tm // 8, 8, tn), axis=0)
        rm_ref[at, :] = mass
        rl_ref[at, :] = load

    groups = rows // LANES
    for g in range(groups):
        gs = slice(g * LANES, (g + 1) * LANES)
        rows_ref[g : g + 1, :] = gather_rows(rm_ref[gs, :])
        rows_ref[groups + g : groups + g + 1, :] = gather_rows(rl_ref[gs, :])
    tiles = cols // LANES
    for t in range(tiles):
        ts = slice(t * LANES, (t + 1) * LANES)
        cols_ref[t : t + 1, :] = jnp.sum(cm_ref[:, ts], axis=0, keepdims=True)
        cols_ref[tiles + t : tiles + t + 1, :] = jnp.sum(cl_ref[:, ts], axis=0, keepdims=True)


def columns_of(plan_ref, scales, spread_ref, out_ref):
    rows, cols = plan_ref.shape
    tiles = cols // LANES
    count = len(scales)
    for k, scale in enumerate(scales):
        for g in range(rows // LANES):
            spread_ref[k, g * LANES : (g + 1) * LANES, :] = spread_rows(scale[g : g + 1, :])
    wide = 16
    for t0 in range(0, tiles, wide):
        span = min(wide, tiles - t0)

        def step(i, acc, t0=t0, span=span):
            acc = list(acc)
            for r in range(8):
                at = pl.ds(pl.multiple_of(i * 64 + r * 8, 8), 8)
                scale_rows = [spread_ref[k, at, :] for k in range(count)]
                for t in range(span):
                    tile = plan_ref[at, (t0 + t) * LANES : (t0 + t + 1) * LANES]
                    for k in range(count):
                        acc[k * span + t] = acc[k * span + t] + tile * scale_rows[k]
            return tuple(acc)

        zero = jnp.zeros((8, LANES), F32)
        acc = lax.fori_loop(0, rows // 64, step, (zero,) * (count * span))
        for k in range(count):
            for t in range(span):
                at = k * tiles + t0 + t
                out_ref[at : at + 1, :] = jnp.sum(acc[k * span + t], axis=0, keepdims=True)


def rows_of(plan_ref, scales, part_ref, out_ref):
    rows, cols = plan_ref.shape
    tiles = cols // LANES
    groups = rows // LANES
    count = len(scales)
    spread = [
        [jnp.broadcast_to(scale[t : t + 1, :], (8, LANES)) for t in range(tiles)] for scale in scales
    ]

    @pl.loop(0, rows // 64)
    def _(i):
        for r in range(8):
            at = pl.ds(pl.multiple_of(i * 64 + r * 8, 8), 8)
            sums = [[None, None] for _ in range(count)]
            for t in range(tiles):
                tile = plan_ref[at, t * LANES : (t + 1) * LANES]
                for k in range(count):
                    term = tile * spread[k][t]
                    old = sums[k][t % 2]
                    sums[k][t % 2] = term if old is None else old + term
            for k in range(count):
                one, two = sums[k]
                part_ref[k, at, :] = one if two is None else one + two

    for k in range(count):
        for g in range(groups):
            at = k * groups + g
            out_ref[at : at + 1, :] = gather_rows(part_ref[k, g * LANES : (g + 1) * LANES, :])


def second_kernel(plan_ref, rows_ref, cols_ref, out_ref, own_ref, spread_ref):
    groups = rows_ref.shape[0] // 2
    tiles = own_ref.shape[0]
    scale = rows_ref[groups:, :] / rows_ref[:groups, :]
    columns_of(plan_ref, [scale], spread_ref, own_ref)
    out_ref[: 2 * tiles, :] = cols_ref[...]
    out_ref[2 * tiles :, :] = own_ref[...]


def third_kernel(plan_ref, cols_ref, out_ref, part_ref):
    tiles = cols_ref.shape[0] // 3
    mass = cols_ref[:tiles, :]
    load = cols_ref[tiles : 2 * tiles, :]
    beta = load - cols_ref[2 * tiles :, :]
    rows_of(plan_ref, [load / mass, beta / mass], part_ref, out_ref)


def fourth_kernel(plan_ref, rows_ref, terms_ref, out_ref, spread_ref):
    groups = rows_ref.shape[0] // 2
    mass = rows_ref[:groups, :]
    load = rows_ref[groups:, :]
    scales = [(load - terms_ref[k * groups : (k + 1) * groups, :]) / mass for k in range(2)]
    columns_of(plan_ref, scales, spread_ref, out_ref)


def fifth_kernel(plan_ref, cols_ref, terms_ref, out_ref, part_ref):
    tiles = cols_ref.shape[0] // 3
    beta = cols_ref[tiles : 2 * tiles, :] - terms_ref[:tiles, :]
    rows_of(plan_ref, [beta / cols_ref[:tiles, :]], part_ref, out_ref)


def weights_of(plan_ref, cot_ref, spread_ref, low, at, js):
    tn = js.stop - js.start
    spread = spread_ref[at, :]
    tm = spread.shape[0]
    shift = jnp.tile(spread, (1, tn // LANES)).reshape(tm // 8, 8, tn) + low[None]
    return split2(plan_ref[at, js] * (cot_ref[at, js] - shift.reshape(tm, tn)))


def right_of(cen_ref, right_ref):
    ch, cl = split2(cen_ref[...])
    transpose_into(right_ref, jnp.concatenate([ch.astype(F32), cl.astype(F32)], axis=0))


def fold_into(out_ref, at, total):
    flipped = total.T
    out_ref[:, at] = flipped[: LANES // 2] + flipped[LANES // 2 :]


def bary_kernel(plan_ref, cen_ref, out_ref, right_ref):
    right_of(cen_ref, right_ref)
    for g in range(plan_ref.shape[0] // LANES):
        at = slice(g * LANES, (g + 1) * LANES)
        both = jnp.concatenate(split2(plan_ref[at, :]), axis=0)
        total = dot(both, right_ref[...])
        fold_into(out_ref, at, total[:LANES] + total[LANES:])


def pre_kernel(plan_ref, cot_ref, right_ref, cols_ref, bterms_ref, out_ref, beta_ref):
    tiles = cols_ref.shape[0] // 3
    beta = (cols_ref[tiles : 2 * tiles, :] - bterms_ref[tiles:, :]) / cols_ref[:tiles, :]
    for t in range(tiles):
        beta_ref[:, t * LANES : (t + 1) * LANES] = jnp.broadcast_to(beta[t : t + 1, :], (8, LANES))
    cols = plan_ref.shape[1]
    low = beta_ref[...][None]
    for g in range(plan_ref.shape[0] // LANES):
        at = slice(g * LANES, (g + 1) * LANES)
        shifted = cot_ref[at, :].reshape(LANES // 8, 8, cols) - low
        both = jnp.concatenate(split2(plan_ref[at, :] * shifted.reshape(LANES, cols)), axis=0)
        total = dot(both, right_ref[...])
        fold_into(out_ref, at, total[:LANES] + total[LANES:])


def post_kernel(pre_ref, bary_ref, rows_ref, aterms_ref, keep_ref, send_ref, alpha_ref, flat_ref):
    groups = rows_ref.shape[0] // 2
    alpha_ref[...] = (rows_ref[groups:, :] - aterms_ref[...]) / rows_ref[:groups, :]
    flat_row(alpha_ref[...], flat_ref)
    half, _, span = keep_ref.shape
    me = lax.axis_index("cen") & (half - 1)
    for q in range(2 * half):
        at = pl.ds(pl.multiple_of((me ^ reverse_bits(q, 2 * half)) * span, span), span)
        to_ref = keep_ref if q < half else send_ref
        to_ref[q % half] = pre_ref[:, at] - flat_ref[:, at] * bary_ref[:, at]


def cen_kernel(plan_ref, cot_ref, emb_ref, alpha_ref, beta_ref, gcen_ref, spread_ref):
    rows, cols = plan_ref.shape
    for g in range(rows // LANES):
        spread_ref[g * LANES : (g + 1) * LANES, :] = spread_rows(alpha_ref[g : g + 1, :])
    left = jnp.concatenate(split2(emb_ref[...]), axis=0)
    tn = 256
    tm = 256
    chunks, width, chunk_cols = gcen_ref.shape
    me = lax.axis_index("pts")
    for j in range(cols // tn):
        js = slice(j * tn, (j + 1) * tn)
        gcen = jnp.zeros((2 * width, tn), F32)
        for i in range(rows // tm):
            at = slice(i * tm, (i + 1) * tm)
            wh, wl = weights_of(plan_ref, cot_ref, spread_ref, beta_ref[:, js], at, js)
            gcen = gcen + dot(left[:, at], wh) + dot(left[:, at], wl)
        gcen = gcen[:width] + gcen[width:]
        span = min(chunk_cols, tn)
        for s in range(tn // span):
            col = j * tn + s * span
            gcen_ref[reverse_bits(me ^ (col // chunk_cols), chunks), :, pl.ds(col % chunk_cols, span)] = gcen[
                :, s * span : (s + 1) * span
            ]


def last_kernel(own_ref, got_ref, mine_ref, theirs_ref, emb_ref, cen_ref):
    half, _, span = own_ref.shape
    chunks = 2 * half
    me = lax.axis_index("cen") & (half - 1)
    for q in range(chunks):
        place = me ^ reverse_bits(q, chunks)
        at = pl.ds(pl.multiple_of(place * span, span), span)
        from_ref = own_ref if q < half else got_ref
        emb_ref[:, at] = from_ref[q % half]
    cen_ref[...] = mine_ref[...] + theirs_ref[...]


def swap(value, axis, count, bit):
    return lax.ppermute(value, axis, [(i, i ^ bit) for i in range(count)])


def sum_all(value, axis, count, first):
    bits = bits_of(count)
    groups = [bits[:first]] + [bits[at : at + 2] for at in range(first, len(bits), 2)]
    for group in groups:
        if len(group) == 1:
            value = value + swap(value, axis, count, group[0])
        else:
            one, two = group
            near = swap(value, axis, count, one)
            far = swap(value, axis, count, two)
            both = swap(value, axis, count, one + two)
            value = (value + near) + (far + both)
    return value


def shards(embeddings, centroids, point_duals, centroid_duals, targets):
    pts = lax.axis_size("pts")
    cen = lax.axis_size("cen")
    rows, width = embeddings.shape
    cols = centroids.shape[0]
    emb, tgt, ctr = embeddings.T, targets.T, centroids.T
    groups, tiles = rows // LANES, cols // LANES
    sds = jax.ShapeDtypeStruct

    def call(body, outs, scratch, mib, specs, *args, flops=1 << 30):
        return pl.pallas_call(
            body,
            out_shape=outs,
            in_specs=specs,
            out_specs=jax.tree.map(lambda _: VMEM, outs),
            scratch_shapes=scratch,
            cost_estimate=pl.CostEstimate(flops=flops, transcendentals=0, bytes_accessed=1 << 20),
            compiler_params=pltpu.CompilerParams(vmem_limit_bytes=mib << 20),
        )(*args)

    def first(*args):
        return first_kernel(float(cols * cen), *args)

    plan, cot, row_sums, col_sums = call(
        first,
        (
            pltpu.VMEM((rows, cols), F32),
            pltpu.VMEM((rows, cols), F32),
            pltpu.VMEM((2 * groups, LANES), F32),
            pltpu.VMEM((2 * tiles, LANES), F32),
        ),
        [
            pltpu.VMEM((width, rows), F32),
            pltpu.VMEM((width, rows), F32),
            pltpu.VMEM((width, cols), F32),
            pltpu.VMEM((groups, LANES), F32),
            pltpu.VMEM((tiles, LANES), F32),
            pltpu.SemaphoreType.DMA((5,)),
            pltpu.VMEM((2, rows, 2 * LANES), BF16),
            pltpu.VMEM((2 * LANES, cols), BF16),
            pltpu.VMEM((rows, LANES), F32),
            pltpu.VMEM((rows, LANES), F32),
            pltpu.VMEM((8, cols), F32),
            pltpu.VMEM((8, cols), F32),
            pltpu.VMEM((1, rows), F32),
            pltpu.VMEM((1, cols), F32),
        ],
        24,
        [pl.BlockSpec(memory_space=pltpu.HBM)] * 5,
        *(
            pltpu.with_memory_space_constraint(x, pltpu.HBM)
            for x in (emb, tgt, ctr, point_duals.reshape(groups, LANES), centroid_duals.reshape(tiles, LANES))
        ),
    )
    row_sums = sum_all(row_sums, "cen", cen, 2)
    col_all = call(
        second_kernel,
        pltpu.VMEM((3 * tiles, LANES), F32),
        [pltpu.VMEM((tiles, LANES), F32), pltpu.VMEM((1, rows, LANES), F32)],
        6,
        [VMEM] * 3,
        plan,
        row_sums,
        col_sums,
    )
    col_all = sum_all(col_all, "pts", pts, 1)
    row_terms = call(
        third_kernel,
        pltpu.VMEM((2 * groups, LANES), F32),
        [pltpu.VMEM((2, rows, LANES), F32)],
        6,
        [VMEM] * 2,
        plan,
        col_all,
    )
    bary, right = call(
        bary_kernel,
        (pltpu.VMEM((width, rows), F32), pltpu.VMEM((cols, LANES), BF16)),
        [],
        12,
        [VMEM] * 2,
        plan,
        ctr,
    )
    row_terms = sum_all(row_terms, "cen", cen, 2)
    col_terms = call(
        fourth_kernel,
        pltpu.VMEM((2 * tiles, LANES), F32),
        [pltpu.VMEM((2, rows, LANES), F32)],
        6,
        [VMEM] * 3,
        plan,
        row_sums,
        row_terms,
    )
    col_terms = sum_all(col_terms, "pts", pts, 1)
    last_terms = call(
        fifth_kernel,
        pltpu.VMEM((groups, LANES), F32),
        [pltpu.VMEM((1, rows, LANES), F32)],
        6,
        [VMEM] * 3,
        plan,
        col_all,
        col_terms,
    )
    pre, beta = call(
        pre_kernel,
        (pltpu.VMEM((width, rows), F32), pltpu.VMEM((8, cols), F32)),
        [],
        12,
        [VMEM] * 5,
        plan,
        cot,
        right,
        col_all,
        col_terms,
    )
    last_terms = sum_all(last_terms, "cen", cen, 2)
    gemb, sent, alpha = call(
        post_kernel,
        (
            pltpu.VMEM((cen // 2, width, rows // cen), F32),
            pltpu.VMEM((cen // 2, width, rows // cen), F32),
            pltpu.VMEM((groups, LANES), F32),
        ),
        [pltpu.VMEM((1, rows), F32)],
        6,
        [VMEM] * 4,
        pre,
        bary,
        row_sums,
        last_terms,
    )
    sent = swap(sent, "cen", cen, 1)
    gcen = call(
        cen_kernel,
        pltpu.VMEM((pts, width, cols // pts), F32),
        [pltpu.VMEM((rows, LANES), F32)],
        12,
        [VMEM] * 5,
        plan,
        cot,
        emb,
        alpha,
        beta,
        flops=1 << 33,
    )
    cbits, pbits = bits_of(cen), bits_of(pts)
    gemb = gemb + sent
    for bit in cbits[1:-1]:
        keep = gemb.shape[0] // 2
        gemb = gemb[:keep] + swap(gemb[keep:], "cen", cen, bit)
    gemb = gemb + swap(gemb, "cen", cen, cbits[-1])
    for bit in reversed(cbits[1:-1]):
        gemb = jnp.concatenate([gemb, swap(gemb, "cen", cen, bit)], axis=0)
    got = swap(gemb, "cen", cen, cbits[0])
    for bit in pbits[:-1]:
        keep = gcen.shape[0] // 2
        gcen = gcen[:keep] + swap(gcen[keep:], "pts", pts, bit)
    theirs = swap(gcen[1], "pts", pts, pbits[-1])
    grad_emb, grad_cen = call(
        last_kernel,
        (sds((width, rows), F32), sds((width, cols // pts), F32)),
        [],
        6,
        [VMEM] * 4,
        gemb,
        got,
        gcen[0],
        theirs,
    )
    return grad_emb.T, grad_cen.T


def solution(mesh):
    in_specs = (P("pts", None), P("cen", None), P("pts"), P("cen"), P("pts", None))
    out_specs = (P("pts", None), P(("cen", "pts"), None))
    return jax.shard_map(shards, mesh=mesh, in_specs=in_specs, out_specs=out_specs, check_vma=False)
```

```python
import math

import jax
import jax.numpy as jnp
from jax import lax
from jax.experimental import pallas as pl
from jax.experimental.pallas import tpu as pltpu
from jax.sharding import PartitionSpec as P


EPSILON = 0.08
LANES = 128
LOG2_E = math.log2(math.e)
F32 = jnp.float32
BF16 = jnp.bfloat16
VMEM = pl.BlockSpec(memory_space=pltpu.VMEM)


def bits_of(count):
    return [1 << b for b in range(count.bit_length() - 1)]


def reverse_bits(k, count):
    size = len(bits_of(count))
    return sum(((k >> b) & 1) << (size - 1 - b) for b in range(size))


def split2(x):
    high = x.astype(BF16)
    low = (x - high.astype(F32)).astype(BF16)
    return high, low


def split3(x):
    high = x.astype(BF16)
    rest = x - high.astype(F32)
    mid = rest.astype(BF16)
    low = (rest - mid.astype(F32)).astype(BF16)
    return high, mid, low


def dot(a, b):
    return jnp.dot(a, b, preferred_element_type=F32)


def flat_row(blocks, out_ref):
    for g in range(blocks.shape[0]):
        out_ref[:, g * LANES : (g + 1) * LANES] = blocks[g : g + 1, :]


def transpose_into(out_ref, source, out_at=0):
    for g in range(source.shape[1] // LANES):
        gs = slice(g * LANES, (g + 1) * LANES)
        out_ref[gs, out_at : out_at + source.shape[0]] = source[:, gs].T.astype(out_ref.dtype)


def spread_rows(row):
    return jnp.broadcast_to(row, (LANES, LANES)).T


def gather_rows(block):
    return jnp.sum(block.T, axis=0, keepdims=True)


def dual_rows(dual, own_first):
    high, mid, low = (part.astype(F32) for part in split3(dual))
    at = lax.broadcasted_iota(jnp.int32, (8, dual.shape[1]), 0)
    first = 0 if own_first else 3
    ones = jnp.where(at < 6, 1.0, 0.0)
    rows = jnp.where(
        at == first, high, jnp.where(at == first + 1, mid, jnp.where(at == first + 2, low, ones))
    )
    return jnp.concatenate([rows, jnp.zeros((56, dual.shape[1]), F32)], axis=0)


def first_kernel(total, emb_hbm, tgt_hbm, cen_hbm, pd_hbm, cd_hbm, plan_ref, cot_ref, rows_ref, cols_ref,
                 emb_ref, tgt_ref, cen_ref, pd_ref, cd_ref, sems, lhs_ref, rhs_ref, rm_ref, rl_ref, cm_ref, cl_ref, pdual_ref, cdual_ref):
    rows, cols = plan_ref.shape
    copies = [
        pltpu.make_async_copy(source, target, sems.at[k])
        for k, (source, target) in enumerate(
            [(cen_hbm, cen_ref), (cd_hbm, cd_ref), (emb_hbm, emb_ref), (pd_hbm, pd_ref), (tgt_hbm, tgt_ref)]
        )
    ]
    for copy in copies:
        copy.start()
    cm_ref[...] = jnp.zeros_like(cm_ref)
    cl_ref[...] = jnp.zeros_like(cl_ref)
    for copy in copies:
        copy.wait()
    flat_row(pd_ref[...] * LOG2_E, pdual_ref)
    flat_row(cd_ref[...] * LOG2_E - math.log2(total), cdual_ref)
    eh, el = (part.astype(F32) for part in split2(emb_ref[...] * (LOG2_E / EPSILON)))
    th, tl = (part.astype(F32) for part in split2(tgt_ref[...]))
    transpose_into(lhs_ref.at[0], jnp.concatenate([eh, eh], axis=0))
    transpose_into(lhs_ref.at[0], jnp.concatenate([el, dual_rows(pdual_ref[...], True)], axis=0), LANES)
    transpose_into(lhs_ref.at[1], jnp.concatenate([th, th], axis=0))
    transpose_into(lhs_ref.at[1], jnp.concatenate([tl, jnp.zeros_like(tl)], axis=0), LANES)
    ch, cl = split2(cen_ref[...])
    rhs_ref[...] = jnp.concatenate([ch, cl, ch, dual_rows(cdual_ref[...], False).astype(BF16)], axis=0)
    tm, tn = 128, 256

    @pl.loop(0, rows // tm)
    def _(i):
        at = pl.ds(pl.multiple_of(i * tm, tm), tm)
        left = lhs_ref[:, at, :].reshape(2 * tm, 2 * LANES)
        mass = jnp.zeros((tm, LANES), F32)
        load = jnp.zeros((tm, LANES), F32)
        for j in range(cols // tn):
            js = slice(j * tn, (j + 1) * tn)
            right = rhs_ref[:, js]
            both = dot(left, right)
            plan = jnp.exp2(both[:tm])
            cot = both[tm:]
            plan_ref[at, js] = plan
            cot_ref[at, js] = cot
            weighted = plan * cot
            for h in range(tn // LANES):
                hs = slice(h * LANES, (h + 1) * LANES)
                mass = mass + plan[:, hs]
                load = load + weighted[:, hs]
            cm_ref[:, js] += jnp.sum(plan.reshape(tm // 8, 8, tn), axis=0)
            cl_ref[:, js] += jnp.sum(weighted.reshape(tm // 8, 8, tn), axis=0)
        rm_ref[at, :] = mass
        rl_ref[at, :] = load

    groups = rows // LANES
    for g in range(groups):
        gs = slice(g * LANES, (g + 1) * LANES)
        rows_ref[g : g + 1, :] = gather_rows(rm_ref[gs, :])
        rows_ref[groups + g : groups + g + 1, :] = gather_rows(rl_ref[gs, :])
    tiles = cols // LANES
    for t in range(tiles):
        ts = slice(t * LANES, (t + 1) * LANES)
        cols_ref[t : t + 1, :] = jnp.sum(cm_ref[:, ts], axis=0, keepdims=True)
        cols_ref[tiles + t : tiles + t + 1, :] = jnp.sum(cl_ref[:, ts], axis=0, keepdims=True)


def columns_of(plan_ref, scales, spread_ref, out_ref):
    rows, cols = plan_ref.shape
    tiles = cols // LANES
    count = len(scales)
    for k, scale in enumerate(scales):
        for g in range(rows // LANES):
            spread_ref[k, g * LANES : (g + 1) * LANES, :] = spread_rows(scale[g : g + 1, :])
    wide = 16
    for t0 in range(0, tiles, wide):
        span = min(wide, tiles - t0)

        def step(i, acc, t0=t0, span=span):
            acc = list(acc)
            for r in range(8):
                at = pl.ds(pl.multiple_of(i * 64 + r * 8, 8), 8)
                scale_rows = [spread_ref[k, at, :] for k in range(count)]
                for t in range(span):
                    tile = plan_ref[at, (t0 + t) * LANES : (t0 + t + 1) * LANES]
                    for k in range(count):
                        acc[k * span + t] = acc[k * span + t] + tile * scale_rows[k]
            return tuple(acc)

        zero = jnp.zeros((8, LANES), F32)
        acc = lax.fori_loop(0, rows // 64, step, (zero,) * (count * span))
        for k in range(count):
            for t in range(span):
                at = k * tiles + t0 + t
                out_ref[at : at + 1, :] = jnp.sum(acc[k * span + t], axis=0, keepdims=True)


def rows_of(plan_ref, scales, part_ref, out_ref):
    rows, cols = plan_ref.shape
    tiles = cols // LANES
    groups = rows // LANES
    count = len(scales)
    spread = [
        [jnp.broadcast_to(scale[t : t + 1, :], (8, LANES)) for t in range(tiles)] for scale in scales
    ]

    @pl.loop(0, rows // 64)
    def _(i):
        for r in range(8):
            at = pl.ds(pl.multiple_of(i * 64 + r * 8, 8), 8)
            sums = [[None, None] for _ in range(count)]
            for t in range(tiles):
                tile = plan_ref[at, t * LANES : (t + 1) * LANES]
                for k in range(count):
                    term = tile * spread[k][t]
                    old = sums[k][t % 2]
                    sums[k][t % 2] = term if old is None else old + term
            for k in range(count):
                one, two = sums[k]
                part_ref[k, at, :] = one if two is None else one + two

    for k in range(count):
        for g in range(groups):
            at = k * groups + g
            out_ref[at : at + 1, :] = gather_rows(part_ref[k, g * LANES : (g + 1) * LANES, :])


def second_kernel(plan_ref, rows_ref, cols_ref, out_ref, own_ref, spread_ref):
    groups = rows_ref.shape[0] // 2
    tiles = own_ref.shape[0]
    scale = rows_ref[groups:, :] / rows_ref[:groups, :]
    columns_of(plan_ref, [scale], spread_ref, own_ref)
    out_ref[: 2 * tiles, :] = cols_ref[...]
    out_ref[2 * tiles :, :] = own_ref[...]


def third_kernel(plan_ref, cols_ref, out_ref, part_ref):
    tiles = cols_ref.shape[0] // 3
    mass = cols_ref[:tiles, :]
    load = cols_ref[tiles : 2 * tiles, :]
    beta = load - cols_ref[2 * tiles :, :]
    rows_of(plan_ref, [load / mass, beta / mass], part_ref, out_ref)


def fourth_kernel(plan_ref, rows_ref, terms_ref, out_ref, spread_ref):
    groups = rows_ref.shape[0] // 2
    mass = rows_ref[:groups, :]
    load = rows_ref[groups:, :]
    scales = [(load - terms_ref[k * groups : (k + 1) * groups, :]) / mass for k in range(2)]
    columns_of(plan_ref, scales, spread_ref, out_ref)


def fifth_kernel(plan_ref, cols_ref, terms_ref, out_ref, part_ref):
    tiles = cols_ref.shape[0] // 3
    beta = cols_ref[tiles : 2 * tiles, :] - terms_ref[:tiles, :]
    rows_of(plan_ref, [beta / cols_ref[:tiles, :]], part_ref, out_ref)


def weights_of(plan_ref, cot_ref, spread_ref, low, at, js):
    tn = js.stop - js.start
    spread = spread_ref[at, :]
    tm = spread.shape[0]
    shift = jnp.tile(spread, (1, tn // LANES)).reshape(tm // 8, 8, tn) + low[None]
    return split2(plan_ref[at, js] * (cot_ref[at, js] - shift.reshape(tm, tn)))


def right_of(cen_ref, right_ref):
    ch, cl = split2(cen_ref[...])
    transpose_into(right_ref, jnp.concatenate([ch.astype(F32), cl.astype(F32)], axis=0))


def fold_into(out_ref, at, total):
    flipped = total.T
    out_ref[:, at] = flipped[: LANES // 2] + flipped[LANES // 2 :]


def bary_kernel(plan_ref, cen_ref, out_ref, right_ref):
    right_of(cen_ref, right_ref)
    for g in range(plan_ref.shape[0] // LANES):
        at = slice(g * LANES, (g + 1) * LANES)
        both = jnp.concatenate(split2(plan_ref[at, :]), axis=0)
        total = dot(both, right_ref[...])
        fold_into(out_ref, at, total[:LANES] + total[LANES:])


def pre_kernel(plan_ref, cot_ref, right_ref, cols_ref, bterms_ref, out_ref, beta_ref):
    tiles = cols_ref.shape[0] // 3
    beta = (cols_ref[tiles : 2 * tiles, :] - bterms_ref[tiles:, :]) / cols_ref[:tiles, :]
    for t in range(tiles):
        beta_ref[:, t * LANES : (t + 1) * LANES] = jnp.broadcast_to(beta[t : t + 1, :], (8, LANES))
    cols = plan_ref.shape[1]
    low = beta_ref[...][None]
    for g in range(plan_ref.shape[0] // LANES):
        at = slice(g * LANES, (g + 1) * LANES)
        shifted = cot_ref[at, :].reshape(LANES // 8, 8, cols) - low
        both = jnp.concatenate(split2(plan_ref[at, :] * shifted.reshape(LANES, cols)), axis=0)
        total = dot(both, right_ref[...])
        fold_into(out_ref, at, total[:LANES] + total[LANES:])


def post_kernel(pre_ref, bary_ref, rows_ref, aterms_ref, *out_refs):
    *piece_refs, alpha_ref, flat_ref = out_refs
    groups = rows_ref.shape[0] // 2
    alpha_ref[...] = (rows_ref[groups:, :] - aterms_ref[...]) / rows_ref[:groups, :]
    flat_row(alpha_ref[...], flat_ref)
    quarter, _, span = piece_refs[0].shape
    half = 2 * quarter
    me = lax.axis_index("cen") & (half - 1)
    for q in range(2 * half):
        at = pl.ds(pl.multiple_of((me ^ reverse_bits(q, 2 * half)) * span, span), span)
        to_ref = piece_refs[q % 2 if q < half else 2 + q % 2]
        to_ref[q % half // 2] = pre_ref[:, at] - flat_ref[:, at] * bary_ref[:, at]


def cen_kernel(plan_ref, cot_ref, emb_ref, alpha_ref, beta_ref, gcen_ref, spread_ref):
    rows, cols = plan_ref.shape
    for g in range(rows // LANES):
        spread_ref[g * LANES : (g + 1) * LANES, :] = spread_rows(alpha_ref[g : g + 1, :])
    left = jnp.concatenate(split2(emb_ref[...]), axis=0)
    tn = 256
    tm = 256
    chunks, width, chunk_cols = gcen_ref.shape
    me = lax.axis_index("pts")
    for j in range(cols // tn):
        js = slice(j * tn, (j + 1) * tn)
        gcen = jnp.zeros((2 * width, tn), F32)
        for i in range(rows // tm):
            at = slice(i * tm, (i + 1) * tm)
            wh, wl = weights_of(plan_ref, cot_ref, spread_ref, beta_ref[:, js], at, js)
            gcen = gcen + dot(left[:, at], wh) + dot(left[:, at], wl)
        gcen = gcen[:width] + gcen[width:]
        span = min(chunk_cols, tn)
        for s in range(tn // span):
            col = j * tn + s * span
            gcen_ref[reverse_bits(me ^ (col // chunk_cols), chunks), :, pl.ds(col % chunk_cols, span)] = gcen[
                :, s * span : (s + 1) * span
            ]


def last_kernel(*refs):
    *piece_refs, mine_ref, theirs_ref, emb_ref, cen_ref = refs
    quarter, _, span = piece_refs[0].shape
    half = 2 * quarter
    me = lax.axis_index("cen") & (half - 1)
    for q in range(2 * half):
        place = me ^ reverse_bits(q, 2 * half)
        at = pl.ds(pl.multiple_of(place * span, span), span)
        from_ref = piece_refs[q % 2 if q < half else 2 + q % 2]
        emb_ref[:, at] = from_ref[q % half // 2]
    cen_ref[...] = mine_ref[...] + theirs_ref[...]


def swap(value, axis, count, bit):
    return lax.ppermute(value, axis, [(i, i ^ bit) for i in range(count)])


def sum_all(value, axis, count, first):
    bits = bits_of(count)
    groups = [bits[:first]] + [bits[at : at + 2] for at in range(first, len(bits), 2)]
    for group in groups:
        if len(group) == 1:
            value = value + swap(value, axis, count, group[0])
        else:
            one, two = group
            near = swap(value, axis, count, one)
            far = swap(value, axis, count, two)
            both = swap(value, axis, count, one + two)
            value = (value + near) + (far + both)
    return value


def shards(embeddings, centroids, point_duals, centroid_duals, targets):
    pts = lax.axis_size("pts")
    cen = lax.axis_size("cen")
    rows, width = embeddings.shape
    cols = centroids.shape[0]
    emb, tgt, ctr = embeddings.T, targets.T, centroids.T
    groups, tiles = rows // LANES, cols // LANES
    sds = jax.ShapeDtypeStruct

    def call(body, outs, scratch, mib, specs, *args, flops=1 << 30):
        return pl.pallas_call(
            body,
            out_shape=outs,
            in_specs=specs,
            out_specs=jax.tree.map(lambda _: VMEM, outs),
            scratch_shapes=scratch,
            cost_estimate=pl.CostEstimate(flops=flops, transcendentals=0, bytes_accessed=1 << 20),
            compiler_params=pltpu.CompilerParams(vmem_limit_bytes=mib << 20),
        )(*args)

    def first(*args):
        return first_kernel(float(cols * cen), *args)

    plan, cot, row_sums, col_sums = call(
        first,
        (
            pltpu.VMEM((rows, cols), F32),
            pltpu.VMEM((rows, cols), F32),
            pltpu.VMEM((2 * groups, LANES), F32),
            pltpu.VMEM((2 * tiles, LANES), F32),
        ),
        [
            pltpu.VMEM((width, rows), F32),
            pltpu.VMEM((width, rows), F32),
            pltpu.VMEM((width, cols), F32),
            pltpu.VMEM((groups, LANES), F32),
            pltpu.VMEM((tiles, LANES), F32),
            pltpu.SemaphoreType.DMA((5,)),
            pltpu.VMEM((2, rows, 2 * LANES), BF16),
            pltpu.VMEM((2 * LANES, cols), BF16),
            pltpu.VMEM((rows, LANES), F32),
            pltpu.VMEM((rows, LANES), F32),
            pltpu.VMEM((8, cols), F32),
            pltpu.VMEM((8, cols), F32),
            pltpu.VMEM((1, rows), F32),
            pltpu.VMEM((1, cols), F32),
        ],
        24,
        [pl.BlockSpec(memory_space=pltpu.HBM)] * 5,
        *(
            pltpu.with_memory_space_constraint(x, pltpu.HBM)
            for x in (emb, tgt, ctr, point_duals.reshape(groups, LANES), centroid_duals.reshape(tiles, LANES))
        ),
    )
    row_sums = sum_all(row_sums, "cen", cen, 2)
    col_all = call(
        second_kernel,
        pltpu.VMEM((3 * tiles, LANES), F32),
        [pltpu.VMEM((tiles, LANES), F32), pltpu.VMEM((1, rows, LANES), F32)],
        6,
        [VMEM] * 3,
        plan,
        row_sums,
        col_sums,
    )
    col_all = sum_all(col_all, "pts", pts, 1)
    row_terms = call(
        third_kernel,
        pltpu.VMEM((2 * groups, LANES), F32),
        [pltpu.VMEM((2, rows, LANES), F32)],
        6,
        [VMEM] * 2,
        plan,
        col_all,
    )
    bary, right = call(
        bary_kernel, (pltpu.VMEM((width, rows), F32), pltpu.VMEM((cols, LANES), BF16)), [], 12, [VMEM] * 2, plan, ctr
    )
    row_terms = sum_all(row_terms, "cen", cen, 2)
    col_terms = call(
        fourth_kernel,
        pltpu.VMEM((2 * tiles, LANES), F32),
        [pltpu.VMEM((2, rows, LANES), F32)],
        6,
        [VMEM] * 3,
        plan,
        row_sums,
        row_terms,
    )
    col_terms = sum_all(col_terms, "pts", pts, 1)
    last_terms = call(
        fifth_kernel,
        pltpu.VMEM((groups, LANES), F32),
        [pltpu.VMEM((1, rows, LANES), F32)],
        6,
        [VMEM] * 3,
        plan,
        col_all,
        col_terms,
    )
    pre, beta = call(
        pre_kernel,
        (pltpu.VMEM((width, rows), F32), pltpu.VMEM((8, cols), F32)),
        [],
        12,
        [VMEM] * 5,
        plan,
        cot,
        right,
        col_all,
        col_terms,
    )
    last_terms = sum_all(last_terms, "cen", cen, 2)
    *pieces, alpha = call(
        post_kernel,
        (pltpu.VMEM((cen // 4, width, rows // cen), F32),) * 4 + (pltpu.VMEM((groups, LANES), F32),),
        [pltpu.VMEM((1, rows), F32)],
        6,
        [VMEM] * 4,
        pre,
        bary,
        row_sums,
        last_terms,
    )
    even = swap(pieces[2], "cen", cen, 1)
    odd = swap(pieces[3], "cen", cen, 1)
    gcen = call(
        cen_kernel,
        pltpu.VMEM((pts, width, cols // pts), F32),
        [pltpu.VMEM((rows, LANES), F32)],
        12,
        [VMEM] * 5,
        plan,
        cot,
        emb,
        alpha,
        beta,
        flops=1 << 33,
    )
    cbits, pbits = bits_of(cen), bits_of(pts)
    owns, gots = [], []
    for own, sent in ((pieces[0], even), (pieces[1], odd)):
        own = own + sent
        for bit in cbits[1:-1]:
            keep = own.shape[0] // 2
            own = own[:keep] + swap(own[keep:], "cen", cen, bit)
        own = own + swap(own, "cen", cen, cbits[-1])
        for bit in reversed(cbits[1:-1]):
            own = jnp.concatenate([own, swap(own, "cen", cen, bit)], axis=0)
        owns.append(own)
        gots.append(swap(own, "cen", cen, cbits[0]))
    for bit in pbits[:-1]:
        keep = gcen.shape[0] // 2
        gcen = gcen[:keep] + swap(gcen[keep:], "pts", pts, bit)
    theirs = swap(gcen[1], "pts", pts, pbits[-1])
    grad_emb, grad_cen = call(
        last_kernel,
        (sds((width, rows), F32), sds((width, cols // pts), F32)),
        [],
        6,
        [VMEM] * 6,
        *owns,
        *gots,
        gcen[0],
        theirs,
    )
    return grad_emb.T, grad_cen.T


def solution(mesh):
    in_specs = (P("pts", None), P("cen", None), P("pts"), P("cen"), P("pts", None))
    out_specs = (P("pts", None), P(("cen", "pts"), None))
    return jax.shard_map(shards, mesh=mesh, in_specs=in_specs, out_specs=out_specs, check_vma=False)
```
